128 devices in a mesh: attn: 8 (over x, core), ffn: 16 (over y, z).
Axes of the slice: x: 4, y: 4, z: 4, core: 2. Of those that a mesh axis runs over, the one named last changes fastest.
Arguments:
- queries: bfloat16 [1024, 2, 64, 576], P(('attn', 'ffn')), may hold values from -9 to 9
- latent_cache: bfloat16 [1024, 512, 576], P(('attn', 'ffn')), may hold values from -4 to 4
- fresh_latent: bfloat16 [1024, 2, 576], P(('attn', 'ffn')), may hold values from -4 to 4
- lengths: int32 [1024], P(('attn', 'ffn')), may hold values from 1 to 512, 262144 in all
- handoff: int32 [16, 8], P('ffn'), may hold values 0 or 1
- residual: bfloat16 [1024, 2, 7168], P(('attn', 'ffn')), may hold values from -30 to 30
- value_up_matrix: bfloat16 [64, 512, 128], P('ffn'), may hold values from -0.5 to 0.5
- output_weight: bfloat16 [8192, 7168], P('ffn'), may hold values from -0.1875 to 0.1875
- norm_gain: float32 [7168], replicated, may hold values from 0.3 to 3
- router: bfloat16 [7168, 16], replicated, may hold values from -0.0625 to 0.0625
- expert_ids: int32 [1024, 2, 2], P('attn'), may hold values from 0 to 15, all different within a row; in each aligned block of 256 rows (0 to 255, 256 to 511, ..., all dimensions but the last counted through in order) at most 64 rows name the same one
- gate_weight: bfloat16 [16, 7168, 2048], P('ffn', None, 'attn'), may hold values from -0.0625 to 0.0625
- up_weight: bfloat16 [16, 7168, 2048], P('ffn', None, 'attn'), may hold values from -0.0625 to 0.0625
- down_weight: bfloat16 [16, 2048, 7168], P('ffn', 'attn'), may hold values from -0.125 to 0.125
Outputs:
- attended: bfloat16 [1024, 2, 7168], P(('attn', 'ffn'))
- expert_out: bfloat16 [1024, 2, 7168], P(('attn', 'ffn'))
The draws below stay inside these ranges and needn't reach their ends.
Inputs may be any that keep to these rules, and one draw needn't show every extreme that they name: `expert_ids`: the 2 ids of a token differ. In each aligned block of 256 tokens (the requests of one index of attn, all new tokens of each, in order) no expert is chosen by more than 64 tokens, and some expert is chosen by exactly 64 in some block.
All inputs are finite; a program needn't handle non-finite values. No bound on the sum of `lengths` or of `handoff` on one device may be relied on, other than what follows from the above.
Results may differ from the reference program's by a relative error of at most 0.014.
Values may be sent and summed in bfloat16 or wider, within the bound.
A program may use at most 128 MiB of HBM per device.

```python
import math
import jax
import jax.numpy as jnp
import numpy as np
from jax import lax

D = 7168
HEADS = 64
KV_RANK = 512
LATENT = 576
V_HEAD = 128
EXP_W = 2048
TOP = 2
STEPS = 2
LEN = 512
REQ_DEV = 8
EXPERTS = 16
REQS = 1024
ROW_REQ = 128
CAP = 64
N_ATTN = 8
N_FFN = 16


def leading_rows(key):
    base_key = jax.random.fold_in(key, 4101)
    return jax.random.truncated_normal(base_key, -4.0, 4.0, (REQS, 2, LATENT), jnp.float32)


def draw_latent_cache(key, part):
    front_rows = leading_rows(key)
    later_key = jax.random.fold_in(key, 4102)
    later_rows = jax.random.truncated_normal(later_key, -4.0, 4.0, (REQS, LEN - 2, LATENT), jnp.float32)
    return jnp.concatenate([front_rows, later_rows], axis=1).astype(jnp.bfloat16)


def draw_queries(key, part):
    base_key = jax.random.fold_in(key, 4201)
    shape_full = (REQS, STEPS, HEADS, LATENT)
    value_rows = jax.random.truncated_normal(base_key, -4.0, 4.0, shape_full, jnp.float32)
    return value_rows.astype(jnp.bfloat16)


def draw_residual(key, part):
    base_key = jax.random.fold_in(key, 4301)
    log_ten = math.log(10.0)
    per_row_scale = jnp.exp(jax.random.uniform(jax.random.fold_in(base_key, 1), (REQS, STEPS, 1), jnp.float32, 0.0, log_ten))
    column_scale = jnp.exp(jax.random.uniform(jax.random.fold_in(base_key, 2), (1, 1, D), jnp.float32, 0.0, log_ten))
    random_part = jax.random.truncated_normal(jax.random.fold_in(base_key, 4), -3.0, 3.0, (REQS, STEPS, D), jnp.float32)
    return (random_part * per_row_scale * column_scale * 0.1).astype(jnp.bfloat16)


def set_ends(drawn, key, smallest, high):
    spot = [jax.random.randint(jax.random.fold_in(key, axis), (), 0, length) for axis, length in enumerate(drawn.shape)]
    main_axis = drawn.shape.index(max(drawn.shape))
    neighbour = spot[:main_axis] + [(spot[main_axis] + 1) % drawn.shape[main_axis]] + spot[main_axis + 1:]
    return drawn.at[tuple(spot)].set(smallest).at[tuple(neighbour)].set(high)


def block_levels(stream_key, dims, split, smallest, largest):
    gain, own = 1.0, jax.random.fold_in(stream_key, 6)
    for dim, shards_of in split:
        heights = jnp.exp(jax.random.uniform(jax.random.fold_in(own, dim), (shards_of,), jnp.float32, smallest / len(split), largest / len(split)))
        gain = gain * jnp.repeat(heights, dims[dim] // shards_of).reshape([-1 if axis == dim else 1 for axis in range(len(dims))])
    return gain


def profile(count, total, reach, slope):
    weights = [(1 << 20) // math.isqrt(rank ** slope) + 1 for rank in range(2, count + 1)]
    rest, holding = total - reach - (count - 1), [1] * (count - 1)
    while rest > 0:
        candidates = [i for i in range(count - 1) if holding[i] < reach]
        pool, left = sum([weights[i] for i in candidates]), rest
        for i in candidates:
            addition = min(reach - holding[i], max(1, left * weights[i] // pool), rest)
            holding[i] = holding[i] + addition
            rest = rest - addition
    return np.array([reach] + holding)


def ragged_sizes(key, count, total, bound, lean):
    if count == 2:
        one = jax.random.randint(key, (), max(1, total - bound), min(bound, total - 1) + 1)
        return jnp.stack([one, total - one])
    sizes = jnp.asarray(profile(count, total, bound, lean), jnp.int32)
    pairs = (count - 1) // 2
    source_of, taker = sizes[1:1 + 2 * pairs:2], sizes[2:2 + 2 * pairs:2]
    slack = jnp.minimum(source_of - 1, bound - taker)
    passed = jax.random.randint(jax.random.fold_in(key, 1), (pairs,), 0, 1 << 20) % (slack + 1)
    sizes = sizes.at[1:1 + 2 * pairs:2].set(source_of - passed).at[2:2 + 2 * pairs:2].set(taker + passed)
    return sizes[jax.random.permutation(jax.random.fold_in(key, 2), count)]


def routed_block(rng, own, number, rows, count, top, reach, skew):
    sequence = jax.random.permutation(rng, count)
    crowded, usual = load_shares(count, rows * top, reach, skew, True), load_shares(count, rows * top, reach, skew, False)
    places = jnp.arange(count)

    def named(sizes, offset_by):
        used = int((sizes > 0).sum())
        fixed = max(1, used // 4)
        shifted = fixed + (places - fixed + offset_by * (used - fixed)) % max(1, count - fixed)
        return jnp.zeros((count,), jnp.int32).at[sequence[jnp.where(places < fixed, places, shifted)]].set(jnp.asarray(sizes, jnp.int32))

    sizes = jnp.where(number % 4 == 0, named(crowded, number // 4), named(usual, number - number // 4 - 1))
    mixed = jax.random.permutation(jax.random.fold_in(own, 3), count)
    donor, sink = mixed[0:count // 2 * 2:2], mixed[1:count // 2 * 2:2]
    room = jnp.minimum(sizes[donor] - 1, reach - sizes[sink]) // 2
    room = jnp.where((donor == sequence[0]) | (sink == sequence[0]) | (sizes[sink] == 0), 0, jnp.maximum(room, 0))
    shifted = jax.random.randint(jax.random.fold_in(own, 4), (count // 2,), 0, 1 << 20) % (room + 1)
    sizes = sizes.at[donor].add(-shifted).at[sink].add(shifted)
    labels = jnp.searchsorted(jnp.cumsum(sizes), jnp.arange(rows * top), side="right").astype(jnp.int32)
    table = labels.reshape(top, rows).T
    table = table[jax.random.permutation(jax.random.fold_in(own, 1), rows)]
    offset_by = jax.random.randint(jax.random.fold_in(own, 2), (rows, 1), 0, top)
    return jnp.take_along_axis(table, (jnp.arange(top)[None, :] + offset_by) % top, axis=1)


def load_shares(count, total, most, slope, full):
    portions = [(1 << 20) // math.isqrt(standing ** slope) + 1 for standing in range(1, count + 1)]
    largest = most if full else min(most, max(-(-total // count), total * portions[0] // sum(portions)))
    least = 1 if total - largest >= count - 1 else 0
    holding, surplus = [largest] + [least] * (count - 1), total - largest - least * (count - 1)
    while surplus > 0:
        movable = [i for i in range(1, count) if holding[i] < largest] or [i for i in range(1, count) if holding[i] < most]
        pool, remaining = sum([portions[i] for i in movable]), surplus
        for i in movable:
            extra = min(most - holding[i], max(1, remaining * portions[i] // pool), surplus)
            holding[i] = holding[i] + extra
            surplus = surplus - extra
    return np.array(holding)


def centred(rng, dims, spread, bound, pieces=(), kind=jnp.bfloat16):
    array = spread * jax.random.normal(rng, dims, jnp.float32)
    if pieces:
        array = array * block_levels(rng, dims, pieces, -0.22, 0.18)
    return jnp.clip(array, -bound, bound).astype(kind)


def setup_inputs(seed: int = 0) -> dict:
    streams_of = jax.random.split(jax.random.key(seed), 15)
    queries = draw_queries(jax.random.fold_in(streams_of[14], 71), 0)
    latent_cache = draw_latent_cache(jax.random.fold_in(streams_of[14], 71), 0)
    fresh_latent = centred(streams_of[2], (REQS, STEPS, LATENT), 1.0, 4.0, ((0, 128),))
    lengths = ragged_sizes(streams_of[3], REQS, REQS * LEN // 2, LEN, 2).astype(jnp.int32)
    handoff = set_ends((jax.random.randint(streams_of[4], (N_FFN, REQ_DEV), 0, 2) < 1).astype(jnp.int32), jax.random.fold_in(streams_of[4], 1), 0, 1)
    residual = draw_residual(jax.random.fold_in(streams_of[14], 71), 0)
    value_up_matrix = centred(streams_of[6], (HEADS, KV_RANK, V_HEAD), (KV_RANK // 4) ** -0.5, 0.5, ((0, 16),))
    output_weight = centred(streams_of[7], (HEADS * V_HEAD, D), (HEADS * V_HEAD // 8) ** -0.5, 0.1875, ((0, 16),))
    norm_gain = jnp.clip(jnp.exp(jax.random.uniform(streams_of[8], (D,), jnp.float32, math.log(0.3), math.log(3.0))), 0.3, 3.0)
    router = centred(streams_of[9], (D, EXPERTS), D ** -0.5, 0.0625)
    expert_ids_keys = jax.random.split(jax.random.fold_in(streams_of[10], 1), REQS * STEPS // (ROW_REQ * STEPS))
    expert_ids_turns = jax.random.permutation(jax.random.fold_in(streams_of[10], 3), REQS * STEPS // (ROW_REQ * STEPS))
    expert_ids = jax.vmap(lambda own, number: routed_block(jax.random.fold_in(streams_of[10], 2), own, number, ROW_REQ * STEPS, EXPERTS, TOP, CAP, 2))(expert_ids_keys, expert_ids_turns).reshape((REQS, STEPS, TOP))
    gate_weight = centred(streams_of[11], (EXPERTS, D, EXP_W), D ** -0.5, 0.0625, ((0, 16), (2, 8)))
    up_weight = centred(streams_of[12], (EXPERTS, D, EXP_W), D ** -0.5, 0.0625, ((0, 16), (2, 8)))
    down_weight = centred(streams_of[13], (EXPERTS, EXP_W, D), EXP_W ** -0.5, 0.125, ((0, 16), (1, 8)))
    return dict(queries=queries, latent_cache=latent_cache, fresh_latent=fresh_latent, lengths=lengths, handoff=handoff, residual=residual, value_up_matrix=value_up_matrix, output_weight=output_weight, norm_gain=norm_gain, router=router, expert_ids=expert_ids, gate_weight=gate_weight, up_weight=up_weight, down_weight=down_weight)


score_scale = 192.0 ** (-0.5)
norm_epsilon = 1e-06

def attend_one(item):
    queries, latent_cache, fresh_latent, sequence_length = item
    rows_flat = queries.reshape(STEPS * HEADS, LATENT)
    old_scores = jnp.dot(rows_flat, latent_cache.T, preferred_element_type=jnp.float32) * score_scale
    position = jnp.arange(LEN, dtype=jnp.int32)
    old_scores = jnp.where(position[None, :] < sequence_length, old_scores, -jnp.inf)
    new_scores = jnp.dot(rows_flat, fresh_latent.T, preferred_element_type=jnp.float32) * score_scale
    row_step = jnp.arange(STEPS * HEADS, dtype=jnp.int32) // HEADS
    column_step = jnp.arange(STEPS, dtype=jnp.int32)
    new_scores = jnp.where(column_step[None, :] <= row_step[:, None], new_scores, -jnp.inf)
    row_peak = jnp.maximum(lax.optimization_barrier(jnp.max(old_scores, axis=1)), lax.optimization_barrier(jnp.max(new_scores, axis=1)))[:, None]
    old_exp = jnp.exp(old_scores - row_peak)
    new_exp = jnp.exp(new_scores - row_peak)
    denominator = lax.optimization_barrier(jnp.sum(old_exp, axis=1, keepdims=True)) + lax.optimization_barrier(jnp.sum(new_exp, axis=1, keepdims=True))
    old_probs = (old_exp / denominator).astype(jnp.bfloat16)
    new_probs = (new_exp / denominator).astype(jnp.bfloat16)
    latent_mix = jnp.dot(old_probs, latent_cache[:, :KV_RANK], preferred_element_type=jnp.float32)
    latent_mix = latent_mix + jnp.dot(new_probs, fresh_latent[:, :KV_RANK], preferred_element_type=jnp.float32)
    return latent_mix.astype(jnp.bfloat16).reshape(STEPS, HEADS, KV_RANK)

def reference(queries, latent_cache, fresh_latent, lengths, handoff, residual, value_up_matrix, output_weight, norm_gain, router, expert_ids, gate_weight, up_weight, down_weight):
    latent_out = lax.map(attend_one, (queries, latent_cache, fresh_latent, lengths))
    grid = latent_out.reshape(N_ATTN, N_FFN, REQ_DEV, STEPS, HEADS, KV_RANK)
    rolled = jnp.roll(grid, 1, axis=0)
    placed_tokens = jnp.where(handoff[None, :, :, None, None, None] == 1, rolled, grid)
    placed_tokens = placed_tokens.reshape(REQS, STEPS, HEADS, KV_RANK)
    value_rows = jnp.einsum('olfb,fbw->olfw', placed_tokens.astype(jnp.float32), value_up_matrix.astype(jnp.float32)).astype(jnp.bfloat16)
    token_total = REQS * STEPS
    heads_out = jnp.dot(value_rows.reshape(token_total, HEADS * V_HEAD), output_weight, preferred_element_type=jnp.float32)
    state = residual.reshape(token_total, D).astype(jnp.float32) + heads_out
    attended = state.astype(jnp.bfloat16)
    scale_rows = lax.rsqrt(lax.optimization_barrier(jnp.mean(state * state, axis=1, keepdims=True)) + norm_epsilon)
    normed = (state * scale_rows * norm_gain.astype(jnp.float32)[None, :]).astype(jnp.bfloat16)
    logits = jnp.dot(normed, router, preferred_element_type=jnp.float32)
    affinity = jax.nn.sigmoid(logits)
    ids_flat = expert_ids.reshape(token_total, TOP)
    onehot = ids_flat[:, :, None] == jnp.arange(EXPERTS, dtype=jnp.int32)[None, None, :]
    chosen = lax.optimization_barrier(jnp.sum(jnp.where(onehot, affinity[:, None, :], jnp.float32(0.0)), axis=2))
    gate_fraction_value = 2.5 * chosen / lax.optimization_barrier(jnp.sum(chosen, axis=1, keepdims=True))
    weight_table = lax.optimization_barrier(jnp.sum(jnp.where(onehot, gate_fraction_value[:, :, None], jnp.float32(0.0)), axis=1))
    hit_table = lax.optimization_barrier(jnp.sum(onehot.astype(jnp.int32), axis=1))
    row_tokens = ROW_REQ * STEPS
    normed_blocks = normed.reshape(N_ATTN, row_tokens, D).astype(jnp.float32)
    slot_ids = jnp.arange(CAP, dtype=jnp.int32)

    def one_expert(carry, item):
        expert_index, gate_here, up_here, down_here = item
        token_hit = lax.optimization_barrier(jnp.sum(jnp.where(jnp.arange(EXPERTS, dtype=jnp.int32)[None, :] == expert_index, hit_table, 0), axis=1))
        token_weight = lax.optimization_barrier(jnp.sum(jnp.where(jnp.arange(EXPERTS, dtype=jnp.int32)[None, :] == expert_index, weight_table, jnp.float32(0.0)), axis=1))
        hit_blocks = token_hit.reshape(N_ATTN, row_tokens)
        slot_rank = jnp.cumsum(hit_blocks, axis=1) - 1
        selector = ((hit_blocks[:, None, :] == 1) & (slot_rank[:, None, :] == slot_ids[None, :, None])).astype(jnp.float32)
        expert_input = jnp.einsum('act,atd->acd', selector, normed_blocks).astype(jnp.bfloat16).reshape(N_ATTN * CAP, D)
        gate_part = jnp.dot(expert_input, gate_here, preferred_element_type=jnp.float32)
        up_part = jnp.dot(expert_input, up_here, preferred_element_type=jnp.float32)
        hidden_activations = (jax.nn.silu(gate_part) * up_part).astype(jnp.bfloat16)
        expert_rows = jnp.dot(hidden_activations, down_here, preferred_element_type=jnp.float32).astype(jnp.bfloat16)
        returned = jnp.einsum('act,acd->atd', selector, expert_rows.astype(jnp.float32).reshape(N_ATTN, CAP, D))
        return (carry + returned.reshape(token_total, D) * token_weight[:, None], None)
    initial = jnp.zeros((token_total, D), jnp.float32)
    combined, _ = lax.scan(one_expert, initial, (jnp.arange(EXPERTS, dtype=jnp.int32), gate_weight, up_weight, down_weight))
    expert_out = combined.astype(jnp.bfloat16).reshape(REQS, STEPS, D)
    return (attended.reshape(REQS, STEPS, D), expert_out)
```

```python
import jax
import jax.numpy as jnp
from jax import lax
from jax.sharding import PartitionSpec as P

KV_RANK = 512


score_scale = 192.0 ** (-0.5)
norm_epsilon = 1e-06


def shifted(value, axis, by):
    count = lax.axis_size(axis)
    return lax.ppermute(value, axis, [(i, (i + by) % count) for i in range(count)])


def attend_block(queries, latent_cache, fresh_latent, lengths):
    req_count, steps_here, heads_here, latent_width = queries.shape
    cache_span = latent_cache.shape[1]
    row_count = steps_here * heads_here
    rows_flat = queries.reshape(req_count, row_count, latent_width)
    old_scores = (
        jnp.einsum("rqc,rnc->rqn", rows_flat, latent_cache, preferred_element_type=jnp.float32)
        * score_scale
    )
    position = lax.broadcasted_iota(jnp.int32, (1, 1, cache_span), 2)
    old_scores = jnp.where(position < lengths[:, None, None], old_scores, -jnp.inf)
    new_scores = (
        jnp.einsum("rqc,rjc->rqj", rows_flat, fresh_latent, preferred_element_type=jnp.float32)
        * score_scale
    )
    row_step = lax.broadcasted_iota(jnp.int32, (1, row_count, steps_here), 1) // heads_here
    column_step = lax.broadcasted_iota(jnp.int32, (1, row_count, steps_here), 2)
    new_scores = jnp.where(column_step <= row_step, new_scores, -jnp.inf)
    row_peak = jnp.maximum(jnp.max(old_scores, axis=2), jnp.max(new_scores, axis=2))[:, :, None]
    old_exp = jnp.exp(old_scores - row_peak)
    new_exp = jnp.exp(new_scores - row_peak)
    denominator = jnp.sum(old_exp, axis=2, keepdims=True) + jnp.sum(new_exp, axis=2, keepdims=True)
    old_probs = (old_exp / denominator).astype(jnp.bfloat16)
    new_probs = (new_exp / denominator).astype(jnp.bfloat16)
    latent_mix = jnp.einsum(
        "rqn,rnc->rqc", old_probs, latent_cache[:, :, :KV_RANK], preferred_element_type=jnp.float32
    )
    latent_mix = latent_mix + jnp.einsum(
        "rqj,rjc->rqc", new_probs, fresh_latent[:, :, :KV_RANK], preferred_element_type=jnp.float32
    )
    return latent_mix.astype(jnp.bfloat16).reshape(req_count, steps_here, heads_here, KV_RANK)


def rms_normalize(state, norm_gain):
    scale_rows = lax.rsqrt(jnp.mean(state * state, axis=-1, keepdims=True) + norm_epsilon)
    return (state * scale_rows * norm_gain).astype(jnp.bfloat16)


def local(
    queries,
    latent_cache,
    fresh_latent,
    lengths,
    handoff,
    residual,
    value_up_matrix,
    output_weight,
    norm_gain,
    router,
    expert_ids,
    gate_weight,
    up_weight,
    down_weight,
):
    moved_here = (handoff[0] == 1)[:, None, None, None]
    latent_home = attend_block(queries, latent_cache, fresh_latent, lengths)
    latent_out = jnp.where(moved_here, shifted(latent_home, "attn", 1), latent_home)
    heads_local = value_up_matrix.shape[0]
    model_width = output_weight.shape[1]
    head_weight = output_weight.reshape(heads_local, value_up_matrix.shape[2], model_width)
    value_rows = jnp.einsum(
        "olfb,fbw->olfw",
        lax.all_to_all(latent_out, "ffn", split_axis=2, concat_axis=0, tiled=True),
        value_up_matrix,
        preferred_element_type=jnp.float32,
    ).astype(jnp.bfloat16)
    partial_out = jnp.einsum(
        "rshv,hvd->rsd", value_rows, head_weight, preferred_element_type=jnp.float32
    )
    req_dev = residual.shape[0]
    steps_here = residual.shape[1]
    ffn_index = lax.axis_index("ffn")
    own_state = lax.psum_scatter(
        partial_out.astype(jnp.bfloat16).reshape(-1, model_width),
        "ffn",
        scatter_dimension=0,
        tiled=True,
    ).astype(jnp.float32).reshape(residual.shape) + residual.astype(jnp.float32)
    attended = own_state.astype(jnp.bfloat16)
    normed_own = rms_normalize(own_state, norm_gain)
    row_req = partial_out.shape[0]
    normed_rows = lax.all_gather(
        normed_own.reshape(req_dev * steps_here, model_width), "ffn", axis=0, tiled=True
    )
    row_tokens = row_req * steps_here
    normed_flat = normed_rows.reshape(row_tokens, model_width)
    expert_count = router.shape[1]
    logits = jnp.dot(normed_flat, router, preferred_element_type=jnp.float32)
    affinity = jax.nn.sigmoid(logits)
    ids_flat = expert_ids.reshape(row_tokens, expert_ids.shape[2])
    onehot = ids_flat[:, :, None] == lax.broadcasted_iota(jnp.int32, (1, 1, expert_count), 2)
    chosen = jnp.sum(jnp.where(onehot, affinity[:, None, :], 0.0), axis=2)
    gate_fraction_value = 2.5 * chosen / jnp.sum(chosen, axis=1, keepdims=True)
    routed_here = ids_flat == ffn_index
    token_weight = jnp.sum(jnp.where(routed_here, gate_fraction_value, 0.0), axis=1)
    token_hit = jnp.sum(routed_here.astype(jnp.int32), axis=1)
    slot_rank = jnp.cumsum(token_hit) - 1
    capacity = 4 * steps_here * req_dev
    slot_ids = lax.broadcasted_iota(jnp.int32, (capacity, row_tokens), 0)
    selector = ((token_hit[None, :] == 1) & (slot_rank[None, :] == slot_ids)).astype(jnp.bfloat16)
    expert_input = jnp.dot(selector, normed_flat, preferred_element_type=jnp.float32).astype(
        jnp.bfloat16
    )
    gate_local = gate_weight[0]
    up_local = up_weight[0]
    down_local = down_weight[0]
    rows_in = lax.all_gather(expert_input, "attn", axis=0, tiled=True)
    gate_part = jnp.dot(rows_in, gate_local, preferred_element_type=jnp.float32)
    up_part = jnp.dot(rows_in, up_local, preferred_element_type=jnp.float32)
    hidden_all = (jax.nn.silu(gate_part) * up_part).astype(jnp.bfloat16)
    rows_in = hidden_all
    expert_rows = lax.psum_scatter(
        jnp.dot(rows_in, down_local, preferred_element_type=jnp.float32).astype(jnp.bfloat16),
        "attn",
        scatter_dimension=0,
        tiled=True,
    )
    returned = (
        jnp.einsum("ct,cd->td", selector, expert_rows, preferred_element_type=jnp.float32)
        * token_weight[:, None]
    )
    summed = lax.psum_scatter(
        returned.astype(jnp.bfloat16), "ffn", scatter_dimension=0, tiled=True
    )
    return (attended, summed.reshape(residual.shape))


def solution(mesh):
    return jax.shard_map(
        local,
        mesh=mesh,
        in_specs=(
            P(("attn", "ffn"), None, None, None),
            P(("attn", "ffn"), None, None),
            P(("attn", "ffn"), None, None),
            P(("attn", "ffn")),
            P("ffn", None),
            P(("attn", "ffn"), None, None),
            P("ffn", None, None),
            P("ffn", None),
            P(),
            P(),
            P("attn", None, None),
            P("ffn", None, "attn"),
            P("ffn", None, "attn"),
            P("ffn", "attn", None),
        ),
        out_specs=(P(("attn", "ffn"), None, None), P(("attn", "ffn"), None, None)),
        check_vma=False,
    )
```

```python
import jax
import jax.numpy as jnp
from jax import lax
from jax.experimental import pallas as pl
from jax.experimental.pallas import tpu as pltpu
from jax.sharding import PartitionSpec as P

KV_RANK = 512


score_scale = 192.0 ** (-0.5)
norm_epsilon = 1e-06


MESH = pl.DeviceIdType.MESH
RING = 4
FLOWS = 8
F32 = jnp.float32
BF16 = jnp.bfloat16


class Wire:
    def __init__(self, send_sem, recv_sem):
        self.send_sem, self.recv_sem = send_sem, recv_sem
        self.copies, self.settled = [], []

    def send(self, src, dst, device):
        i = len(self.copies)
        copy = pltpu.make_async_remote_copy(
            src_ref=src,
            dst_ref=dst,
            send_sem=self.send_sem.at[i],
            recv_sem=self.recv_sem.at[i],
            device_id=device,
            device_id_type=MESH,
        )
        copy.start()
        self.copies.append(copy)
        return copy

    def settle(self, copies):
        for copy in copies:
            copy.wait_send()
            self.settled.append(copy)

    def drain(self):
        self.settle([c for c in self.copies if not any(c is d for d in self.settled)])


class Ring:
    def __init__(self, pos, device):
        self.pos, self.device = pos, device

    def index(self, by):
        return lax.rem(self.pos + by + RING, RING)

    def at(self, by):
        return self.device(self.index(by))


def rings():
    a, f = lax.axis_index("attn"), lax.axis_index("ffn")
    x, core = a // 2, lax.rem(a, 2)
    y, z = f // RING, lax.rem(f, RING)
    ring_x = Ring(x, lambda p: {"attn": p * 2 + core})
    ring_y = Ring(y, lambda p: {"ffn": p * RING + z})
    ring_z = Ring(z, lambda p: {"ffn": y * RING + p})
    return ring_x, ring_y, ring_z, core, {"attn": x * 2 + 1 - core}


def meet(devices):
    barrier = pltpu.get_barrier_semaphore()
    for device in devices:
        pl.semaphore_signal(barrier, inc=1, device_id=device, device_id_type=MESH)
    pl.semaphore_wait(barrier, len(devices))


class Scatter:
    def __init__(self, wire, ring, way, blocks, bufs, q):
        self.wire, self.ring, self.way, self.blocks = wire, ring, way, blocks
        self.relay, self.direct, self.final, self.stage = [b.at[q] for b in bufs]

    def start(self):
        r, s = self.ring, self.way
        self.c_relay = self.wire.send(self.blocks.at[r.index(2)], self.relay, r.at(s))
        self.c_direct = self.wire.send(self.blocks.at[r.index(-s)], self.direct, r.at(-s))

    def middle(self):
        r, s = self.ring, self.way
        self.c_relay.wait_recv()
        total = self.blocks[r.index(s)].astype(F32) + self.relay[...].astype(F32)
        self.stage[...] = total.astype(BF16)
        self.c_final = self.wire.send(self.stage, self.final, r.at(s))

    def finish(self):
        self.c_direct.wait_recv()
        self.c_final.wait_recv()
        return (
            self.blocks[self.ring.pos].astype(F32)
            + self.direct[...].astype(F32)
            + self.final[...].astype(F32)
        )

    def settle(self):
        self.wire.settle([self.c_relay, self.c_direct, self.c_final])


class Gather:
    def __init__(self, wire, ring, way, own, slot):
        self.wire, self.ring, self.way, self.own, self.slot = wire, ring, way, own, slot

    def start(self):
        r, s = self.ring, self.way
        here = self.slot(r.pos)
        self.c_on = self.wire.send(self.own, here, r.at(s))
        self.c_back = self.wire.send(self.own, here, r.at(-s))

    def middle(self):
        r, s = self.ring, self.way
        self.c_on.wait_recv()
        block = self.slot(r.index(-s))
        self.c_far = self.wire.send(block, block, r.at(s))

    def finish(self):
        self.c_back.wait_recv()
        self.c_far.wait_recv()


def way_of(q):
    return 1 if (q // 2) % 2 == 0 else -1


def waves(count, stages):
    for t in range(count + len(stages) - 1):
        for depth, stage in enumerate(stages):
            if 0 <= t - depth < count:
                stage(2 * (t - depth))
                stage(2 * (t - depth) + 1)


def slots_of(ids_ref, me_f, slots):
    half = ids_ref.shape[1]
    tokens = 2 * half
    ids = ids_ref[...].astype(F32).astype(BF16)
    request = lax.broadcasted_iota(jnp.int32, (half, tokens), 0)
    token = lax.broadcasted_iota(jnp.int32, (half, tokens), 1)
    spread = [
        jnp.dot(ids, (token == 2 * request + t).astype(F32).astype(BF16), preferred_element_type=F32)
        for t in range(2)
    ]
    named = [spread[0][k : k + 1] + spread[1][2 + k : 3 + k] for k in range(2)]
    mine = me_f.astype(F32)
    hit = jnp.where((named[0] == mine) | (named[1] == mine), 1.0, 0.0)
    row = lax.broadcasted_iota(jnp.int32, (tokens, tokens), 0)
    column = lax.broadcasted_iota(jnp.int32, (tokens, tokens), 1)
    before = (row <= column).astype(F32).astype(BF16)
    rank = jnp.dot(
        jnp.broadcast_to(hit, (8, tokens)).astype(BF16), before, preferred_element_type=F32
    )[0:1]
    slot = lax.broadcasted_iota(jnp.int32, (slots, tokens), 0).astype(F32)
    sel_yz = jnp.where((rank - 1.0 == slot) & (hit > 0.5), 1.0, 0.0).astype(BF16)
    source = (column % 64) // 16 * 64 + column // 64 * 16 + column % 16
    swap = (row == source).astype(F32).astype(BF16)
    sel_zy = jnp.dot(sel_yz, swap, preferred_element_type=F32).astype(BF16)
    expert = lax.broadcasted_iota(jnp.int32, (RING * RING, tokens), 0).astype(F32)
    chosen = jnp.where((named[0] == expert) | (named[1] == expert), 1.0, 0.0).astype(BF16)
    flags = lax.dot_general(
        sel_yz, chosen, (((1,), (1,)), ((), ())), preferred_element_type=F32
    )
    return sel_yz, sel_zy, flags


def layer_kernel(
    v_ref, wo_hbm, wg_hbm, wu_hbm, wd_hbm, res_ref, gain_ref, router_ref, ids_ref,
    attended_ref, out_ref,
    vt, wo, wgu, wd, state, normed, gathered, picked, selectors, rows_in, total, hidden,
    away, from_pair, px, p1, p2,
    x0, x1, x2, x3, a0, a1, a2, a3, b0, b1, b2, b3, send_sem, recv_sem, load_sem,
):
    ring_x, ring_y, ring_z, core, pair = rings()
    me_f = lax.axis_index("ffn")
    width = wo.shape[1] // FLOWS
    half = wd.shape[0]
    cols = [pl.ds(q * width, width) for q in range(FLOWS)]
    loads = []
    for q in range(FLOWS):
        load = pltpu.make_async_copy(wo_hbm.at[:, cols[q]], wo.at[:, cols[q]], load_sem.at[q])
        load.start()
        loads.append(load)
    late = [
        pltpu.make_async_copy(wg_hbm, wgu.at[:, pl.ds(0, half)], load_sem.at[FLOWS]),
        pltpu.make_async_copy(wu_hbm, wgu.at[:, pl.ds(half, half)], load_sem.at[FLOWS + 1]),
        pltpu.make_async_copy(wd_hbm, wd, load_sem.at[FLOWS + 2]),
    ]
    for load in late:
        load.start()
    for y in range(RING):
        for z in range(RING):
            vt[pl.ds((z * RING + y) * 16, 16), :] = v_ref[pl.ds((y * RING + z) * 16, 16), :]
    meet([ring_x.at(1), ring_x.at(-1), pair, ring_y.at(1), ring_y.at(-1), ring_z.at(1), ring_z.at(-1)])
    wire = Wire(send_sem, recv_sem)
    first = [ring_y if q % 2 == 0 else ring_z for q in range(FLOWS)]
    second = [ring_z if q % 2 == 0 else ring_y for q in range(FLOWS)]
    x_way = [1 if q % 2 == 0 else -1 for q in range(FLOWS)]

    def plane_scatter():
        return (
            [Scatter(wire, first[q], way_of(q), p1.at[q], (a0, a1, a2, a3), q) for q in range(FLOWS)],
            [Scatter(wire, second[q], way_of(q), p2.at[q], (b0, b1, b2, b3), q) for q in range(FLOWS)],
        )

    outer, inner = plane_scatter()
    squares = []

    def begin(q):
        loads[q].wait()
        rows = (v_ref if q % 2 == 0 else vt)[...]
        part = jnp.dot(rows, wo[:, cols[q]], preferred_element_type=F32)
        p1[q] = part.astype(BF16).reshape(RING, 64, width)
        outer[q].start()

    def turn(q):
        p2[q] = outer[q].finish().astype(BF16).reshape(RING, 16, width)
        inner[q].start()

    def close(q):
        own = inner[q].finish() + res_ref[:, cols[q]].astype(F32)
        state[q] = own
        attended_ref[:, cols[q]] = own.astype(BF16)
        squares.append(jnp.sum(own * own, axis=1, keepdims=True))

    waves(
        FLOWS // 2,
        [begin, lambda q: outer[q].middle(), turn, lambda q: inner[q].middle(), close],
    )
    scale = lax.rsqrt(sum(squares) / wo.shape[1] + norm_epsilon)

    small = [
        Gather(
            wire, first[q], way_of(q), normed.at[q],
            lambda p, q=q: gathered.at[q, second[q].pos, p],
        )
        for q in range(FLOWS)
    ]
    large = [
        Gather(
            wire, second[q], way_of(q), gathered.at[q, second[q].pos],
            lambda p, q=q: gathered.at[q, p],
        )
        for q in range(FLOWS)
    ]
    entry = [
        Gather(wire, ring_x, x_way[q], picked.at[q], lambda p, q=q: rows_in.at[q, core, p])
        for q in range(FLOWS)
    ]
    paired = [[] for _ in range(FLOWS)]
    logit_parts = []

    def share(q, by, src=None):
        block = rows_in.at[q, core, ring_x.index(by)]
        paired[q].append(wire.send(block if src is None else src, block, pair))

    def spread(q):
        value = (state[q] * scale * gain_ref[:, cols[q]]).astype(BF16)
        normed[q] = value
        gathered[q, second[q].pos, first[q].pos] = value
        small[q].start()

    def small_middle(q):
        small[q].middle()
        if q == 1:
            sel_yz, sel_zy, flags = slots_of(ids_ref, me_f, picked.shape[1])
            selectors[0] = sel_zy
            selectors[1] = sel_yz
            named.append(flags)

    named = []

    def widen(q):
        small[q].finish()
        large[q].start()

    def enter(q):
        large[q].finish()
        rows = gathered[q].reshape(RING * RING * 16, width)
        mine = jnp.dot(selectors[q % 2], rows, preferred_element_type=F32).astype(BF16)
        picked[q] = mine
        entry[q].start()
        share(q, 0, picked.at[q])
        rows_in[q, core, ring_x.pos] = mine
        logit_parts.append(
            lax.dot_general(
                mine, router_ref[:, cols[q]], (((1,), (1,)), ((), ())), preferred_element_type=F32
            )
        )

    def pass_on(q):
        entry[q].middle()
        share(q, -x_way[q])

    def arrive(q):
        entry[q].finish()
        share(q, x_way[q])
        share(q, 2)

    def absorb(q):
        for copy in paired[q]:
            copy.wait_recv()
        if q == 0:
            late[0].wait()
            late[1].wait()
        for c in range(2):
            block = rows_in[q, c].reshape(RING * picked.shape[1], width)
            part = jnp.dot(block, wgu[cols[q], :], preferred_element_type=F32)
            if q == 0:
                total[c] = part
            else:
                total[c] += part

    waves(
        FLOWS // 2,
        [
            spread, small_middle, widen, lambda q: large[q].middle(),
            enter, pass_on, arrive, absorb,
        ],
    )

    for c in range(2):
        gate, up = total[c, :, pl.ds(0, half)], total[c, :, pl.ds(half, half)]
        hidden[c] = (gate / (1.0 + jnp.exp(-gate)) * up).astype(BF16)
    late[2].wait()

    along = [Scatter(wire, ring_x, x_way[q], px.at[q], (x0, x1, x2, x3), q) for q in range(FLOWS)]
    outer_back, inner_back = plane_scatter()
    crossing = {}
    share_of = []

    def cross(q):
        part = jnp.dot(hidden[1 - core], wd[:, cols[q]], preferred_element_type=F32)
        away[q] = part.astype(BF16)
        crossing[q] = wire.send(away.at[q], from_pair.at[q], pair)

    def begin_back(q):
        part = jnp.dot(hidden[core], wd[:, cols[q]], preferred_element_type=F32)
        crossing[q].wait_recv()
        part = part + from_pair[q].astype(F32)
        px[q] = part.astype(BF16).reshape(RING, picked.shape[1], width)
        along[q].start()
        if q == 1:
            affinity = 1.0 / (1.0 + jnp.exp(-sum(logit_parts)))
            column = lax.broadcasted_iota(jnp.int32, affinity.shape, 1)
            mine = jnp.sum(jnp.where(column == me_f, affinity, 0.0), axis=1, keepdims=True)
            both = jnp.sum(affinity * named[0], axis=1, keepdims=True)
            share_of.append(2.5 * mine / jnp.where(both > 0.0, both, 1.0))

    def combine(q):
        outer[q].settle()
        inner[q].settle()
        rows = along[q].finish().astype(BF16).astype(F32)
        rows = (rows * share_of[0]).astype(BF16)
        back = lax.dot_general(
            selectors[1 - q % 2], rows, (((0,), (0,)), ((), ())), preferred_element_type=F32
        )
        p1[q] = back.astype(BF16).reshape(RING, 64, width)
        outer_back[q].start()

    def turn_back(q):
        p2[q] = outer_back[q].finish().astype(BF16).reshape(RING, 16, width)
        inner_back[q].start()

    def close_back(q):
        out_ref[:, cols[q]] = inner_back[q].finish().astype(BF16)

    waves(
        FLOWS // 2,
        [
            cross, begin_back, lambda q: along[q].middle(), combine,
            lambda q: outer_back[q].middle(), turn_back,
            lambda q: inner_back[q].middle(), close_back,
        ],
    )
    wire.drain()


def vmem_specs(count):
    return [pl.BlockSpec(memory_space=pltpu.VMEM)] * count


def exchange_bufs(rows, width):
    return [pltpu.VMEM((FLOWS, rows, width), BF16)] * 4


PIECE = 16
VMEM_LIMIT = 66 * 1024 * 1000
SENDS = 2


def attend_kernel(
    len_ref, hand_ref, q_hbm, kt_hbm, fresh_ref, w_ref,
    v_ref,
    flag_ref, q, kt, sent, got, flags, values, passed, send_sem, recv_sem, load_sem,
):
    _, ring_y, ring_z, _, _ = rings()
    a, f = lax.axis_index("attn"), lax.axis_index("ffn")
    count = lax.axis_size("attn")
    onward = {"attn": lax.rem(a + 1, count)}
    behind = {"attn": lax.rem(a + count - 1, count)}
    requests, rows, rank = q.shape[0], q.shape[1], w_ref.shape[1]
    heads = rows // 2
    loads = []
    for r in range(requests):
        pair = (
            pltpu.make_async_copy(q_hbm.at[r], q.at[r], load_sem.at[2 * r]),
            pltpu.make_async_copy(kt_hbm.at[r], kt.at[r], load_sem.at[2 * r + 1]),
        )
        for load in pair:
            load.start()
        loads.append(pair)
    offsets = [(dy, dz) for dy in (2, 1, 3, 0) for dz in (2, 1, 3, 0) if (dy, dz) != (0, 0)]

    def peer(dy, dz):
        return ring_y.index(dy) * RING + ring_z.index(dz)

    token = lax.broadcasted_iota(jnp.int32, flag_ref.shape, 0) // 2
    flag = jnp.zeros(flag_ref.shape, F32)
    for r in range(requests):
        flag = jnp.where(token == r, hand_ref[0, r].astype(F32), flag)
    flag_ref[...] = flag.astype(BF16)
    flags[ring_y.pos, ring_z.pos] = flag.astype(BF16)
    meet([{"ffn": peer(dy, dz)} for dy, dz in offsets] + [onward, behind])
    wire = Wire(send_sem, recv_sem)
    flag_copies = {}
    for dy, dz in offsets:
        flag_copies[dy, dz] = wire.send(
            flag_ref, flags.at[ring_y.pos, ring_z.pos], {"ffn": peer(dy, dz)}
        )

    place = lax.broadcasted_iota(jnp.int32, (2 * rows, 2 * rows), 0)
    source = lax.broadcasted_iota(jnp.int32, (2 * rows, 2 * rows), 1)
    wanted = (
        (place % 16) // 8 * rows + (place % 8) // 4 * heads + place // 16 * 4 + place % 4
    )
    order = (source == wanted).astype(F32).astype(BF16)
    position = lax.broadcasted_iota(jnp.int32, (rows, kt.shape[2]), 1)
    step = lax.broadcasted_iota(jnp.int32, (rows, fresh_ref.shape[1]), 0) // heads
    column = lax.broadcasted_iota(jnp.int32, (rows, fresh_ref.shape[1]), 1)
    across = (((1,), (1,)), ((), ()))

    def attend(r):
        for load in loads[r]:
            load.wait()
        old = jnp.dot(q[r], kt[r], preferred_element_type=F32) * score_scale
        old = jnp.where(position < len_ref[r], old, -jnp.inf)
        new = lax.dot_general(q[r], fresh_ref[r], across, preferred_element_type=F32) * score_scale
        new = jnp.where(column <= step, new, -jnp.inf)
        peak = jnp.maximum(
            jnp.max(old, axis=1, keepdims=True), jnp.max(new, axis=1, keepdims=True)
        )
        old, new = jnp.exp(old - peak), jnp.exp(new - peak)
        below = jnp.sum(old, axis=1, keepdims=True) + jnp.sum(new, axis=1, keepdims=True)
        mixed = lax.dot_general(
            (old / below).astype(BF16), kt[r, pl.ds(0, rank), :], across, preferred_element_type=F32
        )
        mixed = mixed + jnp.dot(
            (new / below).astype(BF16), fresh_ref[r, :, pl.ds(0, rank)], preferred_element_type=F32
        )
        return mixed.astype(BF16)

    pairs = requests // 2
    per_send = pairs // SENDS
    copies = {}
    for p in range(pairs):
        both = jnp.concatenate([attend(2 * p), attend(2 * p + 1)], axis=0)
        piece = jnp.dot(order, both, preferred_element_type=F32).astype(BF16)
        sent[:, p] = piece.reshape(RING * RING, PIECE, rank)
        if (p + 1) % per_send == 0:
            part = pl.ds(p + 1 - per_send, per_send)
            for dy, dz in offsets:
                to = peer(dy, dz)
                copies.setdefault(dy, []).append(
                    wire.send(sent.at[to, part], got.at[ring_y.pos, ring_z.pos, part], {"ffn": to})
                )
    got[ring_y.pos, ring_z.pos] = sent[f]

    block_rows = RING * pairs * PIECE
    tokens = block_rows // 4
    gather = (
        lax.broadcasted_iota(jnp.int32, (tokens, block_rows), 1) // 4
        == lax.broadcasted_iota(jnp.int32, (tokens, block_rows), 0)
    ).astype(F32).astype(BF16)
    head = lax.broadcasted_iota(jnp.int32, (block_rows, w_ref.shape[2]), 0) % 4
    shifts = {}
    turns = (0, 1, 3, 2)
    for dy in turns:
        for copy in copies[dy]:
            copy.wait_recv()
        block = ring_y.index(-dy)
        latents = got[block].reshape(block_rows, rank)
        mapped = [
            jnp.where(
                head == j, jnp.dot(latents, w_ref[j], preferred_element_type=F32), 0.0
            ).astype(BF16)
            for j in range(w_ref.shape[0])
        ]
        value = jnp.dot(gather, jnp.concatenate(mapped, axis=1), preferred_element_type=F32)
        values[block] = value.astype(BF16)
        shifts[dy] = wire.send(values.at[block], passed.at[block], onward)
    for dy, dz in offsets:
        flag_copies[dy, dz].wait_recv()
    for dy in turns:
        shifts[dy].wait_recv()
        block = ring_y.index(-dy)
        flag = flags[block].reshape(tokens, flag_ref.shape[1]).astype(F32)
        moved = jnp.concatenate([flag] * (values.shape[2] // flag.shape[1]), axis=1) > 0.5
        v_ref[block] = jnp.where(moved, passed[block].astype(F32), values[block].astype(F32)).astype(BF16)
    wire.drain()


def attend(queries, cache, fresh, lengths, handoff, value_up):
    requests, steps, heads, latent = queries.shape
    span = cache.shape[1]
    per_dev, rank, v_head = value_up.shape
    rows = steps * heads
    plane = RING * RING
    copies = (plane - 1) * (1 + SENDS) + RING
    tokens = RING * requests * steps
    return pl.pallas_call(
        attend_kernel,
        name="attend",
        out_shape=jax.ShapeDtypeStruct((RING, tokens, per_dev * v_head), BF16),
        in_specs=[pl.BlockSpec(memory_space=pltpu.SMEM)] * 2
        + [pl.BlockSpec(memory_space=pl.ANY)] * 2
        + vmem_specs(2),
        out_specs=vmem_specs(1)[0],
        scratch_shapes=[
            pltpu.VMEM((requests * steps, 128), BF16),
            pltpu.VMEM((requests, rows, latent), BF16),
            pltpu.VMEM((requests, latent, span), BF16),
            pltpu.VMEM((plane, requests // 2, PIECE, rank), BF16),
            pltpu.VMEM((RING, RING, requests // 2, PIECE, rank), BF16),
            pltpu.VMEM((RING, RING, requests * steps, 128), BF16),
            pltpu.VMEM((RING, tokens, per_dev * v_head), BF16),
            pltpu.VMEM((RING, tokens, per_dev * v_head), BF16),
            pltpu.SemaphoreType.DMA((copies,)),
            pltpu.SemaphoreType.DMA((copies,)),
            pltpu.SemaphoreType.DMA((2 * requests,)),
        ],
        compiler_params=pltpu.CompilerParams(collective_id=3, has_side_effects=True),
    )(
        lengths,
        handoff,
        queries.reshape(requests, rows, latent),
        jnp.swapaxes(cache, 1, 2),
        fresh,
        value_up,
    )


def layer(v, output_weight, gate, up, down, residual, norm_gain, router_t, ids):
    depth, model_width = output_weight.shape
    width = model_width // FLOWS
    half = down.shape[0]
    tokens, slots = v.shape[0], 4 * residual.shape[0]
    copies = (12 + 7 + 1 + 9) * FLOWS
    return pl.pallas_call(
        layer_kernel,
        name="layer",
        out_shape=(
            jax.ShapeDtypeStruct((tokens // 16, model_width), BF16),
            jax.ShapeDtypeStruct((tokens // 16, model_width), BF16),
        ),
        in_specs=vmem_specs(1) + [pl.BlockSpec(memory_space=pl.ANY)] * 4 + vmem_specs(4),
        out_specs=tuple(vmem_specs(2)),
        scratch_shapes=[
            pltpu.VMEM((tokens, depth), BF16),
            pltpu.VMEM((depth, model_width), BF16),
            pltpu.VMEM((model_width, 2 * half), BF16),
            pltpu.VMEM((half, model_width), BF16),
            pltpu.VMEM((FLOWS, 16, width), F32),
            pltpu.VMEM((FLOWS, 16, width), BF16),
            pltpu.VMEM((FLOWS, RING, RING, 16, width), BF16),
            pltpu.VMEM((FLOWS, slots, width), BF16),
            pltpu.VMEM((2, slots, tokens), BF16),
            pltpu.VMEM((FLOWS, 2, RING, slots, width), BF16),
            pltpu.VMEM((2, RING * slots, 2 * half), F32),
            pltpu.VMEM((2, RING * slots, half), BF16),
            pltpu.VMEM((FLOWS, RING * slots, width), BF16),
            pltpu.VMEM((FLOWS, RING * slots, width), BF16),
            pltpu.VMEM((FLOWS, RING, slots, width), BF16),
            pltpu.VMEM((FLOWS, RING, 64, width), BF16),
            pltpu.VMEM((FLOWS, RING, 16, width), BF16),
            *exchange_bufs(slots, width),
            *exchange_bufs(64, width),
            *exchange_bufs(16, width),
            pltpu.SemaphoreType.DMA((copies,)),
            pltpu.SemaphoreType.DMA((copies,)),
            pltpu.SemaphoreType.DMA((FLOWS + 3,)),
        ],
        compiler_params=pltpu.CompilerParams(
            collective_id=1, has_side_effects=True, vmem_limit_bytes=VMEM_LIMIT
        ),
    )(v, output_weight, gate, up, down, residual, norm_gain, router_t, ids)


def local(
    queries,
    latent_cache,
    fresh_latent,
    lengths,
    handoff,
    residual,
    value_up_matrix,
    output_weight,
    norm_gain,
    router,
    expert_ids,
    gate_weight,
    up_weight,
    down_weight,
):
    heads_local, _, v_head = value_up_matrix.shape
    req_dev, steps_here, model_width = residual.shape
    row_tokens = expert_ids.shape[0] * steps_here
    value_rows = attend(queries, latent_cache, fresh_latent, lengths, handoff, value_up_matrix)
    attended, summed = layer(
        value_rows.reshape(row_tokens, heads_local * v_head),
        output_weight,
        gate_weight[0],
        up_weight[0],
        down_weight[0],
        residual.reshape(req_dev * steps_here, model_width),
        norm_gain.reshape(1, model_width),
        router.T,
        jnp.transpose(expert_ids, (1, 2, 0)).reshape(-1, expert_ids.shape[0]),
    )
    return (attended.reshape(residual.shape), summed.reshape(residual.shape))


def solution(mesh):
    return jax.shard_map(
        local,
        mesh=mesh,
        in_specs=(
            P(("attn", "ffn"), None, None, None),
            P(("attn", "ffn"), None, None),
            P(("attn", "ffn"), None, None),
            P(("attn", "ffn")),
            P("ffn", None),
            P(("attn", "ffn"), None, None),
            P("ffn", None, None),
            P("ffn", None),
            P(),
            P(),
            P("attn", None, None),
            P("ffn", None, "attn"),
            P("ffn", None, "attn"),
            P("ffn", "attn", None),
        ),
        out_specs=(P(("attn", "ffn"), None, None), P(("attn", "ffn"), None, None)),
        check_vma=False,
    )
```

```python
import jax
import jax.numpy as jnp
from jax import lax
from jax.experimental import pallas as pl
from jax.experimental.pallas import tpu as pltpu
from jax.sharding import PartitionSpec as P

KV_RANK = 512


score_scale = 192.0 ** (-0.5)
norm_epsilon = 1e-06


MESH = pl.DeviceIdType.MESH
RING = 4
FLOWS = 14
F32 = jnp.float32
BF16 = jnp.bfloat16


class Wire:
    def __init__(self, send_sem, recv_sem):
        self.send_sem, self.recv_sem = send_sem, recv_sem
        self.copies, self.settled = [], []

    def send(self, src, dst, device):
        i = len(self.copies)
        copy = pltpu.make_async_remote_copy(
            src_ref=src,
            dst_ref=dst,
            send_sem=self.send_sem.at[i],
            recv_sem=self.recv_sem.at[i],
            device_id=device,
            device_id_type=MESH,
        )
        copy.start()
        self.copies.append(copy)
        return copy

    def settle(self, copies):
        for copy in copies:
            copy.wait_send()
            self.settled.append(copy)

    def drain(self):
        self.settle([c for c in self.copies if not any(c is d for d in self.settled)])


class Ring:
    def __init__(self, pos, device):
        self.pos, self.device = pos, device

    def index(self, by):
        return lax.rem(self.pos + by + RING, RING)

    def at(self, by):
        return self.device(self.index(by))


def rings():
    a, f = lax.axis_index("attn"), lax.axis_index("ffn")
    x, core = a // 2, lax.rem(a, 2)
    y, z = f // RING, lax.rem(f, RING)
    ring_x = Ring(x, lambda p: {"attn": p * 2 + core})
    ring_y = Ring(y, lambda p: {"ffn": p * RING + z})
    ring_z = Ring(z, lambda p: {"ffn": y * RING + p})
    return ring_x, ring_y, ring_z, core, {"attn": x * 2 + 1 - core}


def meet(devices):
    barrier = pltpu.get_barrier_semaphore()
    for device in devices:
        pl.semaphore_signal(barrier, inc=1, device_id=device, device_id_type=MESH)
    pl.semaphore_wait(barrier, len(devices))


class Scatter:
    def __init__(self, wire, ring, way, blocks, bufs, q):
        self.wire, self.ring, self.way, self.blocks = wire, ring, way, blocks
        self.relay, self.direct, self.final, self.stage = [b.at[q] for b in bufs]

    def start(self):
        r, s = self.ring, self.way
        self.c_relay = self.wire.send(self.blocks.at[r.index(2)], self.relay, r.at(s))
        self.c_direct = self.wire.send(self.blocks.at[r.index(-s)], self.direct, r.at(-s))

    def middle(self):
        r, s = self.ring, self.way
        self.c_relay.wait_recv()
        total = self.blocks[r.index(s)].astype(F32) + self.relay[...].astype(F32)
        self.stage[...] = total.astype(BF16)
        self.c_final = self.wire.send(self.stage, self.final, r.at(s))

    def finish(self):
        self.c_direct.wait_recv()
        self.c_final.wait_recv()
        return (
            self.blocks[self.ring.pos].astype(F32)
            + self.direct[...].astype(F32)
            + self.final[...].astype(F32)
        )

    def settle(self):
        self.wire.settle([self.c_relay, self.c_direct, self.c_final])


class Gather:
    def __init__(self, wire, ring, way, own, slot):
        self.wire, self.ring, self.way, self.own, self.slot = wire, ring, way, own, slot

    def start(self):
        r, s = self.ring, self.way
        here = self.slot(r.pos)
        self.c_on = self.wire.send(self.own, here, r.at(s))
        self.c_back = self.wire.send(self.own, here, r.at(-s))

    def middle(self):
        r, s = self.ring, self.way
        self.c_on.wait_recv()
        block = self.slot(r.index(-s))
        self.c_far = self.wire.send(block, block, r.at(s))

    def finish(self):
        self.c_back.wait_recv()
        self.c_far.wait_recv()


class Trade:
    def __init__(self, wire, ring, source, target):
        self.wire, self.ring, self.source, self.target = wire, ring, source, target

    def start(self):
        self.copies = [
            self.wire.send(self.source(self.ring.index(k)), self.target(k), self.ring.at(k))
            for k in (2, 1, 3)
        ]

    def finish(self):
        for copy in self.copies:
            copy.wait_recv()

    def settle(self):
        self.wire.settle(self.copies)


def way_of(q, core):
    return (1 if (q // 2) % 2 == 0 else -1) * (1 - 2 * core)


def waves(count, stages):
    for t in range(count + len(stages) - 1):
        for depth, stage in enumerate(stages):
            if stage is not None and 0 <= t - depth < count:
                stage(2 * (t - depth))
                stage(2 * (t - depth) + 1)


def slots_of(ids_ref, me_f, slots):
    half = ids_ref.shape[1]
    tokens = 2 * half
    ids = ids_ref[...].astype(F32).astype(BF16)
    request = lax.broadcasted_iota(jnp.int32, (half, tokens), 0)
    token = lax.broadcasted_iota(jnp.int32, (half, tokens), 1)
    spread = [
        jnp.dot(ids, (token == 2 * request + t).astype(F32).astype(BF16), preferred_element_type=F32)
        for t in range(2)
    ]
    named = [spread[0][k : k + 1] + spread[1][2 + k : 3 + k] for k in range(2)]
    mine = me_f.astype(F32)
    hit = jnp.where((named[0] == mine) | (named[1] == mine), 1.0, 0.0)
    row = lax.broadcasted_iota(jnp.int32, (tokens, tokens), 0)
    column = lax.broadcasted_iota(jnp.int32, (tokens, tokens), 1)
    before = (row <= column).astype(F32).astype(BF16)
    rank = jnp.dot(
        jnp.broadcast_to(hit, (8, tokens)).astype(BF16), before, preferred_element_type=F32
    )[0:1]
    slot = lax.broadcasted_iota(jnp.int32, (slots, tokens), 0).astype(F32)
    sel_yz = jnp.where((rank - 1.0 == slot) & (hit > 0.5), 1.0, 0.0).astype(BF16)
    source = (column % 64) // 16 * 64 + column // 64 * 16 + column % 16
    swap = (row == source).astype(F32).astype(BF16)
    sel_zy = jnp.dot(sel_yz, swap, preferred_element_type=F32).astype(BF16)
    expert = lax.broadcasted_iota(jnp.int32, (RING * RING, tokens), 0).astype(F32)
    chosen = jnp.where((named[0] == expert) | (named[1] == expert), 1.0, 0.0).astype(BF16)
    flags = lax.dot_general(
        sel_yz, chosen, (((1,), (1,)), ((), ())), preferred_element_type=F32
    )
    return sel_yz, sel_zy, flags


def layer_kernel(
    v_ref, wo_hbm, wg_hbm, wu_hbm, wd_hbm, res_ref, gain_ref, router_ref, ids_ref,
    attended_ref, out_ref,
    vt, wo, wgu, wd, normed, scales, gathered, picked, selectors, slot_scales, rows_in, total, hidden,
    away, from_pair, px, p1, p2,
    x0, x1, x2, x3, a0, a1, a2, a3, b1, b2, b3, send_sem, recv_sem, load_sem,
):
    ring_x, ring_y, ring_z, core, pair = rings()
    a, me_f = lax.axis_index("attn"), lax.axis_index("ffn")
    count = lax.axis_size("attn")
    width = wo.shape[1] // FLOWS
    half = wd.shape[0]
    cols = [pl.ds(q * width, width) for q in range(FLOWS)]
    loads = []
    for q in range(FLOWS):
        load = pltpu.make_async_copy(wo_hbm.at[:, cols[q]], wo.at[:, cols[q]], load_sem.at[q])
        load.start()
        loads.append(load)
    late = [
        pltpu.make_async_copy(wg_hbm, wgu.at[:, pl.ds(0, half)], load_sem.at[FLOWS]),
        pltpu.make_async_copy(wu_hbm, wgu.at[:, pl.ds(half, half)], load_sem.at[FLOWS + 1]),
        pltpu.make_async_copy(wd_hbm, wd, load_sem.at[FLOWS + 2]),
    ]
    for load in late:
        load.start()
    for y in range(RING):
        for z in range(RING):
            vt[pl.ds((z * RING + y) * 16, 16), :] = v_ref[pl.ds((y * RING + z) * 16, 16), :]
    column_peers = [{"attn": lax.rem(a + k, count)} for k in range(1, count)]
    plane_peers = [
        {"ffn": ring_y.index(dy) * RING + ring_z.index(dz)}
        for dy in range(RING)
        for dz in range(RING)
        if (dy, dz) != (0, 0)
    ]
    meet(column_peers + plane_peers)
    wire = Wire(send_sem, recv_sem)
    first = [ring_y if q % 2 == 0 else ring_z for q in range(FLOWS)]
    second = [ring_z if q % 2 == 0 else ring_y for q in range(FLOWS)]
    x_way = [1 if q % 2 == 0 else -1 for q in range(FLOWS)]

    def plane_scatter():
        return (
            [Scatter(wire, first[q], way_of(q, core), p1.at[q], (a0, a1, a2, a3), q) for q in range(FLOWS)],
            [
                Trade(
                    wire, second[q],
                    lambda p, q=q: p2.at[q, p],
                    lambda k, q=q: (b1, b2, b3)[k - 1].at[q],
                )
                for q in range(FLOWS)
            ],
        )

    def inner_sum(q, trade):
        trade.finish()
        own = p2[q, second[q].pos].astype(F32)
        return own + b1[q].astype(F32) + b2[q].astype(F32) + b3[q].astype(F32)

    outer, inner = plane_scatter()
    squares, named, own_scale = [], [], []

    def begin(q):
        loads[q].wait()
        rows = (v_ref if q % 2 == 0 else vt)[...]
        part = jnp.dot(rows, wo[:, cols[q]], preferred_element_type=F32)
        p1[q] = part.astype(BF16).reshape(RING, 64, width)
        outer[q].start()

    def turn(q):
        p2[q] = outer[q].finish().astype(BF16).reshape(RING, 16, width)
        inner[q].start()
        if q == 1:
            sel_yz, sel_zy, flags = slots_of(ids_ref, me_f, picked.shape[1])
            selectors[0] = sel_zy
            selectors[1] = sel_yz
            named.append(flags)

    scale_copies, slot_copies = [], []

    def close(q):
        own = inner_sum(q, inner[q]) + res_ref[:, cols[q]].astype(F32)
        attended_ref[:, cols[q]] = own.astype(BF16)
        squares.append(jnp.sum(own * own, axis=1, keepdims=True))
        value = (own * gain_ref[:, cols[q]]).astype(BF16)
        normed[q] = value
        gathered[q, second[q].pos, first[q].pos] = value
        small[q].start()
        if q == FLOWS - 1:
            scale = lax.rsqrt(sum(squares) / wo.shape[1] + norm_epsilon)
            here = scales.at[ring_y.pos, ring_z.pos]
            here[...] = jnp.broadcast_to(scale, here.shape)
            for peer in plane_peers:
                scale_copies.append(wire.send(here, here, peer))

    def scale_slots():
        for copy in scale_copies:
            copy.wait_recv()
        rest = scales[...].reshape(RING * RING * 16, scales.shape[3])
        found = jnp.zeros((picked.shape[1], scales.shape[3]), F32)
        for _ in range(3):
            part = rest.astype(BF16)
            found += jnp.dot(selectors[1], part, preferred_element_type=F32)
            rest = rest - part.astype(F32)
        here = slot_scales.at[core, ring_x.pos]
        here[...] = found
        for peer in column_peers:
            slot_copies.append(wire.send(here, here, peer))
        return found

    small = [
        Trade(
            wire, first[q],
            lambda p, q=q: normed.at[q],
            lambda k, q=q: gathered.at[q, second[q].pos, first[q].pos],
        )
        for q in range(FLOWS)
    ]
    large = [
        Gather(
            wire, second[q], way_of(q, core), gathered.at[q, second[q].pos],
            lambda p, q=q: gathered.at[q, p],
        )
        for q in range(FLOWS)
    ]
    entry = [
        Gather(wire, ring_x, x_way[q], picked.at[q], lambda p, q=q: rows_in.at[q, core, p])
        for q in range(FLOWS)
    ]
    paired = [[] for _ in range(FLOWS)]
    logit_parts = []

    def share(q, by, src=None):
        block = rows_in.at[q, core, ring_x.index(by)]
        paired[q].append(wire.send(block if src is None else src, block, pair))


    def widen(q):
        small[q].finish()
        large[q].start()

    def enter(q):
        large[q].finish()
        rows = gathered[q].reshape(RING * RING * 16, width)
        mine = jnp.dot(selectors[q % 2], rows, preferred_element_type=F32).astype(BF16)
        picked[q] = mine
        entry[q].start()
        share(q, 0, picked.at[q])
        rows_in[q, core, ring_x.pos] = mine
        logit_parts.append(
            lax.dot_general(
                mine, router_ref[:, cols[q]], (((1,), (1,)), ((), ())), preferred_element_type=F32
            )
        )

    def pass_on(q):
        entry[q].middle()
        share(q, -x_way[q])

    def arrive(q):
        entry[q].finish()
        share(q, x_way[q])
        share(q, 2)

    def absorb(q):
        if q == 1:
            own_scale.append(scale_slots())
        for copy in paired[q]:
            copy.wait_recv()
        if q == 0:
            late[0].wait()
            late[1].wait()
        for c in range(2):
            block = rows_in[q, c].reshape(RING * picked.shape[1], width)
            part = jnp.dot(block, wgu[cols[q], :], preferred_element_type=F32)
            if q == 0:
                total[c] = part
            else:
                total[c] += part

    waves(
        FLOWS // 2,
        [
            begin, lambda q: outer[q].middle(), turn, close, widen,
            lambda q: large[q].middle(), enter, pass_on, arrive, absorb,
        ],
    )

    for copy in slot_copies:
        copy.wait_recv()
    for c in range(2):
        scale = slot_scales[c].reshape(RING * picked.shape[1], slot_scales.shape[3])
        scale = jnp.concatenate([scale] * (half // scale.shape[1]), axis=1)
        gate = total[c, :, pl.ds(0, half)] * scale
        up = total[c, :, pl.ds(half, half)] * scale
        hidden[c] = (gate / (1.0 + jnp.exp(-gate)) * up).astype(BF16)
    late[2].wait()

    along = [Scatter(wire, ring_x, x_way[q], px.at[q], (x0, x1, x2, x3), q) for q in range(FLOWS)]
    outer_back, inner_back = plane_scatter()
    crossing = {}
    share_of = []

    def cross(q):
        part = jnp.dot(hidden[1 - core], wd[:, cols[q]], preferred_element_type=F32)
        away[q] = part.astype(BF16)
        crossing[q] = wire.send(away.at[q], from_pair.at[q], pair)

    def begin_back(q):
        part = jnp.dot(hidden[core], wd[:, cols[q]], preferred_element_type=F32)
        crossing[q].wait_recv()
        part = part + from_pair[q].astype(F32)
        px[q] = part.astype(BF16).reshape(RING, picked.shape[1], width)
        along[q].start()
        if q == 1:
            logits = sum(logit_parts) * own_scale[0][:, : router_ref.shape[0]]
            affinity = 1.0 / (1.0 + jnp.exp(-logits))
            column = lax.broadcasted_iota(jnp.int32, affinity.shape, 1)
            mine = jnp.sum(jnp.where(column == me_f, affinity, 0.0), axis=1, keepdims=True)
            both = jnp.sum(affinity * named[0], axis=1, keepdims=True)
            share_of.append(2.5 * mine / jnp.where(both > 0.0, both, 1.0))

    def combine(q):
        outer[q].settle()
        inner[q].settle()
        rows = along[q].finish().astype(BF16).astype(F32)
        rows = (rows * share_of[0]).astype(BF16)
        back = lax.dot_general(
            selectors[1 - q % 2], rows, (((0,), (0,)), ((), ())), preferred_element_type=F32
        )
        p1[q] = back.astype(BF16).reshape(RING, 64, width)
        outer_back[q].start()

    def turn_back(q):
        p2[q] = outer_back[q].finish().astype(BF16).reshape(RING, 16, width)
        inner_back[q].start()

    def close_back(q):
        out_ref[:, cols[q]] = inner_sum(q, inner_back[q]).astype(BF16)

    waves(
        FLOWS // 2,
        [
            cross, begin_back, lambda q: along[q].middle(), combine,
            lambda q: outer_back[q].middle(), turn_back, close_back,
        ],
    )
    wire.drain()


def vmem_specs(count):
    return [pl.BlockSpec(memory_space=pltpu.VMEM)] * count


def exchange_bufs(rows, width):
    return [pltpu.VMEM((FLOWS, rows, width), BF16)] * 4


PIECE = 16
VMEM_LIMIT = 66 * 1024 * 1000
SENDS = 2


def attend_kernel(
    len_ref, hand_ref, q_hbm, kt_hbm, fresh_ref, w_ref,
    v_ref,
    flag_ref, q, kt, sent, got, flags, values, passed, send_sem, recv_sem, load_sem,
):
    _, ring_y, ring_z, _, _ = rings()
    a, f = lax.axis_index("attn"), lax.axis_index("ffn")
    count = lax.axis_size("attn")
    onward = {"attn": lax.rem(a + 1, count)}
    behind = {"attn": lax.rem(a + count - 1, count)}
    requests, rows, rank = q.shape[0], q.shape[1], w_ref.shape[1]
    heads = rows // 2
    loads = []
    for r in range(requests):
        pair = (
            pltpu.make_async_copy(q_hbm.at[r], q.at[r], load_sem.at[2 * r]),
            pltpu.make_async_copy(kt_hbm.at[r], kt.at[r], load_sem.at[2 * r + 1]),
        )
        for load in pair:
            load.start()
        loads.append(pair)
    offsets = [(dy, dz) for dy in (2, 1, 3, 0) for dz in (2, 1, 3, 0) if (dy, dz) != (0, 0)]

    def peer(dy, dz):
        return ring_y.index(dy) * RING + ring_z.index(dz)

    token = lax.broadcasted_iota(jnp.int32, flag_ref.shape, 0) // 2
    flag = jnp.zeros(flag_ref.shape, F32)
    for r in range(requests):
        flag = jnp.where(token == r, hand_ref[0, r].astype(F32), flag)
    flag_ref[...] = flag.astype(BF16)
    flags[ring_y.pos, ring_z.pos] = flag.astype(BF16)
    meet([{"ffn": peer(dy, dz)} for dy, dz in offsets] + [onward, behind])
    wire = Wire(send_sem, recv_sem)
    flag_copies = {}
    for dy, dz in offsets:
        flag_copies[dy, dz] = wire.send(
            flag_ref, flags.at[ring_y.pos, ring_z.pos], {"ffn": peer(dy, dz)}
        )

    place = lax.broadcasted_iota(jnp.int32, (2 * rows, 2 * rows), 0)
    source = lax.broadcasted_iota(jnp.int32, (2 * rows, 2 * rows), 1)
    wanted = (
        (place % 16) // 8 * rows + (place % 8) // 4 * heads + place // 16 * 4 + place % 4
    )
    order = (source == wanted).astype(F32).astype(BF16)
    position = lax.broadcasted_iota(jnp.int32, (rows, kt.shape[2]), 1)
    step = lax.broadcasted_iota(jnp.int32, (rows, fresh_ref.shape[1]), 0) // heads
    column = lax.broadcasted_iota(jnp.int32, (rows, fresh_ref.shape[1]), 1)
    across = (((1,), (1,)), ((), ()))

    def attend(r):
        for load in loads[r]:
            load.wait()
        old = jnp.dot(q[r], kt[r], preferred_element_type=F32) * score_scale
        old = jnp.where(position < len_ref[r], old, -jnp.inf)
        new = lax.dot_general(q[r], fresh_ref[r], across, preferred_element_type=F32) * score_scale
        new = jnp.where(column <= step, new, -jnp.inf)
        peak = jnp.maximum(
            jnp.max(old, axis=1, keepdims=True), jnp.max(new, axis=1, keepdims=True)
        )
        old, new = jnp.exp(old - peak), jnp.exp(new - peak)
        below = jnp.sum(old, axis=1, keepdims=True) + jnp.sum(new, axis=1, keepdims=True)
        mixed = lax.dot_general(
            (old / below).astype(BF16), kt[r, pl.ds(0, rank), :], across, preferred_element_type=F32
        )
        mixed = mixed + jnp.dot(
            (new / below).astype(BF16), fresh_ref[r, :, pl.ds(0, rank)], preferred_element_type=F32
        )
        return mixed.astype(BF16)

    pairs = requests // 2
    per_send = pairs // SENDS
    copies = {}
    for p in range(pairs):
        both = jnp.concatenate([attend(2 * p), attend(2 * p + 1)], axis=0)
        piece = jnp.dot(order, both, preferred_element_type=F32).astype(BF16)
        sent[:, p] = piece.reshape(RING * RING, PIECE, rank)
        if (p + 1) % per_send == 0:
            part = pl.ds(p + 1 - per_send, per_send)
            for dy, dz in offsets:
                to = peer(dy, dz)
                copies.setdefault(dy, []).append(
                    wire.send(sent.at[to, part], got.at[ring_y.pos, ring_z.pos, part], {"ffn": to})
                )
    got[ring_y.pos, ring_z.pos] = sent[f]

    block_rows = RING * pairs * PIECE
    tokens = block_rows // 4
    gather = (
        lax.broadcasted_iota(jnp.int32, (tokens, block_rows), 1) // 4
        == lax.broadcasted_iota(jnp.int32, (tokens, block_rows), 0)
    ).astype(F32).astype(BF16)
    head = lax.broadcasted_iota(jnp.int32, (block_rows, w_ref.shape[2]), 0) % 4
    shifts = {}
    turns = (0, 1, 3, 2)
    for dy in turns:
        for copy in copies[dy]:
            copy.wait_recv()
        block = ring_y.index(-dy)
        latents = got[block].reshape(block_rows, rank)
        mapped = [
            jnp.where(
                head == j, jnp.dot(latents, w_ref[j], preferred_element_type=F32), 0.0
            ).astype(BF16)
            for j in range(w_ref.shape[0])
        ]
        value = jnp.dot(gather, jnp.concatenate(mapped, axis=1), preferred_element_type=F32)
        values[block] = value.astype(BF16)
        shifts[dy] = wire.send(values.at[block], passed.at[block], onward)
    for dy, dz in offsets:
        flag_copies[dy, dz].wait_recv()
    for dy in turns:
        shifts[dy].wait_recv()
        block = ring_y.index(-dy)
        flag = flags[block].reshape(tokens, flag_ref.shape[1]).astype(F32)
        moved = jnp.concatenate([flag] * (values.shape[2] // flag.shape[1]), axis=1) > 0.5
        v_ref[block] = jnp.where(moved, passed[block].astype(F32), values[block].astype(F32)).astype(BF16)
    wire.drain()


def attend(queries, cache, fresh, lengths, handoff, value_up):
    requests, steps, heads, latent = queries.shape
    span = cache.shape[1]
    per_dev, rank, v_head = value_up.shape
    rows = steps * heads
    plane = RING * RING
    copies = (plane - 1) * (1 + SENDS) + RING
    tokens = RING * requests * steps
    return pl.pallas_call(
        attend_kernel,
        name="attend",
        out_shape=jax.ShapeDtypeStruct((RING, tokens, per_dev * v_head), BF16),
        in_specs=[pl.BlockSpec(memory_space=pltpu.SMEM)] * 2
        + [pl.BlockSpec(memory_space=pl.ANY)] * 2
        + vmem_specs(2),
        out_specs=vmem_specs(1)[0],
        scratch_shapes=[
            pltpu.VMEM((requests * steps, 128), BF16),
            pltpu.VMEM((requests, rows, latent), BF16),
            pltpu.VMEM((requests, latent, span), BF16),
            pltpu.VMEM((plane, requests // 2, PIECE, rank), BF16),
            pltpu.VMEM((RING, RING, requests // 2, PIECE, rank), BF16),
            pltpu.VMEM((RING, RING, requests * steps, 128), BF16),
            pltpu.VMEM((RING, tokens, per_dev * v_head), BF16),
            pltpu.VMEM((RING, tokens, per_dev * v_head), BF16),
            pltpu.SemaphoreType.DMA((copies,)),
            pltpu.SemaphoreType.DMA((copies,)),
            pltpu.SemaphoreType.DMA((2 * requests,)),
        ],
        compiler_params=pltpu.CompilerParams(collective_id=3, has_side_effects=True),
    )(
        lengths,
        handoff,
        queries.reshape(requests, rows, latent),
        jnp.swapaxes(cache, 1, 2),
        fresh,
        value_up,
    )


def layer(v, output_weight, gate, up, down, residual, norm_gain, router_t, ids):
    depth, model_width = output_weight.shape
    width = model_width // FLOWS
    half = down.shape[0]
    tokens, slots = v.shape[0], 4 * residual.shape[0]
    copies = (12 + 7 + 1 + 9) * FLOWS + 15 + 7
    return pl.pallas_call(
        layer_kernel,
        name="layer",
        out_shape=(
            jax.ShapeDtypeStruct((tokens // 16, model_width), BF16),
            jax.ShapeDtypeStruct((tokens // 16, model_width), BF16),
        ),
        in_specs=vmem_specs(1) + [pl.BlockSpec(memory_space=pl.ANY)] * 4 + vmem_specs(4),
        out_specs=tuple(vmem_specs(2)),
        scratch_shapes=[
            pltpu.VMEM((tokens, depth), BF16),
            pltpu.VMEM((depth, model_width), BF16),
            pltpu.VMEM((model_width, 2 * half), BF16),
            pltpu.VMEM((half, model_width), BF16),
            pltpu.VMEM((FLOWS, 16, width), BF16),
            pltpu.VMEM((RING, RING, 16, 128), F32),
            pltpu.VMEM((FLOWS, RING, RING, 16, width), BF16),
            pltpu.VMEM((FLOWS, slots, width), BF16),
            pltpu.VMEM((2, slots, tokens), BF16),
            pltpu.VMEM((2, RING, slots, 128), F32),
            pltpu.VMEM((FLOWS, 2, RING, slots, width), BF16),
            pltpu.VMEM((2, RING * slots, 2 * half), F32),
            pltpu.VMEM((2, RING * slots, half), BF16),
            pltpu.VMEM((FLOWS, RING * slots, width), BF16),
            pltpu.VMEM((FLOWS, RING * slots, width), BF16),
            pltpu.VMEM((FLOWS, RING, slots, width), BF16),
            pltpu.VMEM((FLOWS, RING, 64, width), BF16),
            pltpu.VMEM((FLOWS, RING, 16, width), BF16),
            *exchange_bufs(slots, width),
            *exchange_bufs(64, width),
            *exchange_bufs(16, width)[1:],
            pltpu.SemaphoreType.DMA((copies,)),
            pltpu.SemaphoreType.DMA((copies,)),
            pltpu.SemaphoreType.DMA((FLOWS + 3,)),
        ],
        compiler_params=pltpu.CompilerParams(
            collective_id=1, has_side_effects=True, vmem_limit_bytes=VMEM_LIMIT
        ),
    )(v, output_weight, gate, up, down, residual, norm_gain, router_t, ids)


def local(
    queries,
    latent_cache,
    fresh_latent,
    lengths,
    handoff,
    residual,
    value_up_matrix,
    output_weight,
    norm_gain,
    router,
    expert_ids,
    gate_weight,
    up_weight,
    down_weight,
):
    heads_local, _, v_head = value_up_matrix.shape
    req_dev, steps_here, model_width = residual.shape
    row_tokens = expert_ids.shape[0] * steps_here
    value_rows = attend(queries, latent_cache, fresh_latent, lengths, handoff, value_up_matrix)
    attended, summed = layer(
        value_rows.reshape(row_tokens, heads_local * v_head),
        output_weight,
        gate_weight[0],
        up_weight[0],
        down_weight[0],
        residual.reshape(req_dev * steps_here, model_width),
        norm_gain.reshape(1, model_width),
        router.T,
        jnp.transpose(expert_ids, (1, 2, 0)).reshape(-1, expert_ids.shape[0]),
    )
    return (attended.reshape(residual.shape), summed.reshape(residual.shape))


def solution(mesh):
    return jax.shard_map(
        local,
        mesh=mesh,
        in_specs=(
            P(("attn", "ffn"), None, None, None),
            P(("attn", "ffn"), None, None),
            P(("attn", "ffn"), None, None),
            P(("attn", "ffn")),
            P("ffn", None),
            P(("attn", "ffn"), None, None),
            P("ffn", None, None),
            P("ffn", None),
            P(),
            P(),
            P("attn", None, None),
            P("ffn", None, "attn"),
            P("ffn", None, "attn"),
            P("ffn", "attn", None),
        ),
        out_specs=(P(("attn", "ffn"), None, None), P(("attn", "ffn"), None, None)),
        check_vma=False,
    )
```

```python
import jax
import jax.numpy as jnp
from jax import lax
from jax.experimental import pallas as pl
from jax.experimental.pallas import tpu as pltpu
from jax.sharding import PartitionSpec as P

KV_RANK = 512


score_scale = 192.0 ** (-0.5)
norm_epsilon = 1e-06


MESH = pl.DeviceIdType.MESH
RING = 4
FLOWS = 14
F32 = jnp.float32
BF16 = jnp.bfloat16


class Wire:
    def __init__(self, send_sem, recv_sem):
        self.send_sem, self.recv_sem = send_sem, recv_sem
        self.copies, self.settled = [], []

    def send(self, src, dst, device):
        i = len(self.copies)
        copy = pltpu.make_async_remote_copy(
            src_ref=src,
            dst_ref=dst,
            send_sem=self.send_sem.at[i],
            recv_sem=self.recv_sem.at[i],
            device_id=device,
            device_id_type=MESH,
        )
        copy.start()
        self.copies.append(copy)
        return copy

    def settle(self, copies):
        for copy in copies:
            copy.wait_send()
            self.settled.append(copy)

    def drain(self):
        self.settle([c for c in self.copies if not any(c is d for d in self.settled)])


class Ring:
    def __init__(self, pos, device):
        self.pos, self.device = pos, device

    def index(self, by):
        return lax.rem(self.pos + by + RING, RING)

    def at(self, by):
        return self.device(self.index(by))


def rings():
    a, f = lax.axis_index("attn"), lax.axis_index("ffn")
    x, core = a // 2, lax.rem(a, 2)
    y, z = f // RING, lax.rem(f, RING)
    ring_x = Ring(x, lambda p: {"attn": p * 2 + core})
    ring_y = Ring(y, lambda p: {"ffn": p * RING + z})
    ring_z = Ring(z, lambda p: {"ffn": y * RING + p})
    return ring_x, ring_y, ring_z, core, {"attn": x * 2 + 1 - core}


def meet(devices):
    barrier = pltpu.get_barrier_semaphore()
    for device in devices:
        pl.semaphore_signal(barrier, inc=1, device_id=device, device_id_type=MESH)
    pl.semaphore_wait(barrier, len(devices))


class Scatter:
    def __init__(self, wire, ring, way, blocks, bufs, q):
        self.wire, self.ring, self.way, self.blocks = wire, ring, way, blocks
        self.relay, self.direct, self.final, self.stage = [b.at[q] for b in bufs]

    def start(self):
        r, s = self.ring, self.way
        self.c_relay = self.wire.send(self.blocks.at[r.index(2)], self.relay, r.at(s))
        self.c_direct = self.wire.send(self.blocks.at[r.index(-s)], self.direct, r.at(-s))

    def middle(self):
        r, s = self.ring, self.way
        self.c_relay.wait_recv()
        total = self.blocks[r.index(s)].astype(F32) + self.relay[...].astype(F32)
        self.stage[...] = total.astype(BF16)
        self.c_final = self.wire.send(self.stage, self.final, r.at(s))

    def finish(self):
        self.c_direct.wait_recv()
        self.c_final.wait_recv()
        return (
            self.blocks[self.ring.pos].astype(F32)
            + self.direct[...].astype(F32)
            + self.final[...].astype(F32)
        )

    def settle(self):
        self.wire.settle([self.c_relay, self.c_direct, self.c_final])


class Gather:
    def __init__(self, wire, ring, way, own, slot):
        self.wire, self.ring, self.way, self.own, self.slot = wire, ring, way, own, slot

    def start(self):
        r, s = self.ring, self.way
        here = self.slot(r.pos)
        self.c_on = self.wire.send(self.own, here, r.at(s))
        self.c_back = self.wire.send(self.own, here, r.at(-s))

    def middle(self):
        r, s = self.ring, self.way
        self.c_on.wait_recv()
        block = self.slot(r.index(-s))
        self.c_far = self.wire.send(block, block, r.at(s))

    def finish(self):
        self.c_back.wait_recv()
        self.c_far.wait_recv()


class Trade:
    def __init__(self, wire, ring, source, target):
        self.wire, self.ring, self.source, self.target = wire, ring, source, target

    def start(self):
        self.copies = [
            self.wire.send(self.source(self.ring.index(k)), self.target(k), self.ring.at(k))
            for k in (2, 1, 3)
        ]

    def finish(self):
        for copy in self.copies:
            copy.wait_recv()

    def settle(self):
        self.wire.settle(self.copies)


def way_of(q, core):
    return (1 if (q // 2) % 2 == 0 else -1) * (1 - 2 * core)


def waves(count, stages):
    for t in range(count + len(stages) - 1):
        for depth, stage in enumerate(stages):
            if stage is not None and 0 <= t - depth < count:
                stage(2 * (t - depth))
                stage(2 * (t - depth) + 1)


def slots_of(ids_ref, me_f, slots):
    half = ids_ref.shape[1]
    tokens = 2 * half
    ids = ids_ref[...].astype(F32).astype(BF16)
    request = lax.broadcasted_iota(jnp.int32, (half, tokens), 0)
    token = lax.broadcasted_iota(jnp.int32, (half, tokens), 1)
    spread = [
        jnp.dot(ids, (token == 2 * request + t).astype(F32).astype(BF16), preferred_element_type=F32)
        for t in range(2)
    ]
    named = [spread[0][k : k + 1] + spread[1][2 + k : 3 + k] for k in range(2)]
    mine = me_f.astype(F32)
    hit = jnp.where((named[0] == mine) | (named[1] == mine), 1.0, 0.0)
    row = lax.broadcasted_iota(jnp.int32, (tokens, tokens), 0)
    column = lax.broadcasted_iota(jnp.int32, (tokens, tokens), 1)
    before = (row <= column).astype(F32).astype(BF16)
    rank = jnp.dot(
        jnp.broadcast_to(hit, (8, tokens)).astype(BF16), before, preferred_element_type=F32
    )[0:1]
    slot = lax.broadcasted_iota(jnp.int32, (slots, tokens), 0).astype(F32)
    sel_yz = jnp.where((rank - 1.0 == slot) & (hit > 0.5), 1.0, 0.0).astype(BF16)
    source = (column % 64) // 16 * 64 + column // 64 * 16 + column % 16
    swap = (row == source).astype(F32).astype(BF16)
    sel_zy = jnp.dot(sel_yz, swap, preferred_element_type=F32).astype(BF16)
    expert = lax.broadcasted_iota(jnp.int32, (RING * RING, tokens), 0).astype(F32)
    chosen = jnp.where((named[0] == expert) | (named[1] == expert), 1.0, 0.0).astype(BF16)
    flags = lax.dot_general(
        sel_yz, chosen, (((1,), (1,)), ((), ())), preferred_element_type=F32
    )
    return sel_yz, sel_zy, flags


def layer_kernel(
    v_ref, wo_hbm, wg_hbm, wu_hbm, wd_hbm, res_ref, gain_ref, router_ref, ids_ref,
    attended_ref, out_ref,
    vt, wo, wgu, wd, normed, scales, gathered, picked, selectors, slot_scales, rows_in, total, hidden,
    away, from_pair, px, p1, p2,
    x0, x1, x2, x3, a0, a1, a2, a3, b1, b2, b3, send_sem, recv_sem, load_sem,
):
    ring_x, ring_y, ring_z, core, pair = rings()
    a, me_f = lax.axis_index("attn"), lax.axis_index("ffn")
    count = lax.axis_size("attn")
    width = wo.shape[1] // FLOWS
    half = wd.shape[0]
    cols = [pl.ds(q * width, width) for q in range(FLOWS)]
    loads = []
    for q in range(FLOWS):
        load = pltpu.make_async_copy(wo_hbm.at[:, cols[q]], wo.at[:, cols[q]], load_sem.at[q])
        load.start()
        loads.append(load)
    late = [
        pltpu.make_async_copy(wg_hbm, wgu.at[:, pl.ds(0, half)], load_sem.at[FLOWS]),
        pltpu.make_async_copy(wu_hbm, wgu.at[:, pl.ds(half, half)], load_sem.at[FLOWS + 1]),
        pltpu.make_async_copy(wd_hbm, wd, load_sem.at[FLOWS + 2]),
    ]
    for load in late:
        load.start()
    for y in range(RING):
        for z in range(RING):
            vt[pl.ds((z * RING + y) * 16, 16), :] = v_ref[pl.ds((y * RING + z) * 16, 16), :]
    column_peers = [{"attn": lax.rem(a + k, count)} for k in range(1, count)]
    plane_peers = [
        {"ffn": ring_y.index(dy) * RING + ring_z.index(dz)}
        for dy in range(RING)
        for dz in range(RING)
        if (dy, dz) != (0, 0)
    ]
    meet(column_peers + plane_peers)
    wire = Wire(send_sem, recv_sem)
    first = [ring_y if q % 2 == 0 else ring_z for q in range(FLOWS)]
    second = [ring_z if q % 2 == 0 else ring_y for q in range(FLOWS)]
    x_way = [1 if q % 2 == 0 else -1 for q in range(FLOWS)]

    def plane_scatter():
        return (
            [Scatter(wire, first[q], way_of(q, core), p1.at[q], (a0, a1, a2, a3), q) for q in range(FLOWS)],
            [
                Trade(
                    wire, second[q],
                    lambda p, q=q: p2.at[q, p],
                    lambda k, q=q: (b1, b2, b3)[k - 1].at[q],
                )
                for q in range(FLOWS)
            ],
        )

    def inner_sum(q, trade):
        trade.finish()
        own = p2[q, second[q].pos].astype(F32)
        return own + b1[q].astype(F32) + b2[q].astype(F32) + b3[q].astype(F32)

    outer, inner = plane_scatter()
    squares, named, own_scale = [], [], []

    def begin(q):
        loads[q].wait()
        rows = (v_ref if q % 2 == 0 else vt)[...]
        part = jnp.dot(rows, wo[:, cols[q]], preferred_element_type=F32)
        p1[q] = part.astype(BF16).reshape(RING, 64, width)
        outer[q].start()

    def turn(q):
        p2[q] = outer[q].finish().astype(BF16).reshape(RING, 16, width)
        inner[q].start()
        if q == 1:
            sel_yz, sel_zy, flags = slots_of(ids_ref, me_f, picked.shape[1])
            selectors[0] = sel_zy
            selectors[1] = sel_yz
            named.append(flags)

    scale_copies, slot_copies = [], []

    def close(q):
        own = inner_sum(q, inner[q]) + res_ref[:, :, cols[q]].astype(F32).reshape(16, width)
        attended_ref[:, :, cols[q]] = own.reshape(8, 2, width).astype(BF16)
        squares.append(jnp.sum(own * own, axis=1, keepdims=True))
        value = (own * gain_ref[:, cols[q]]).astype(BF16)
        normed[q] = value
        gathered[q, second[q].pos, first[q].pos] = value
        small[q].start()
        if q == FLOWS - 1:
            scale = lax.rsqrt(sum(squares) / wo.shape[1] + norm_epsilon)
            here = scales.at[ring_y.pos, ring_z.pos]
            here[...] = jnp.broadcast_to(scale, here.shape)
            for peer in plane_peers:
                scale_copies.append(wire.send(here, here, peer))

    def scale_slots():
        for copy in scale_copies:
            copy.wait_recv()
        rest = scales[...].reshape(RING * RING * 16, scales.shape[3])
        found = jnp.zeros((picked.shape[1], scales.shape[3]), F32)
        for _ in range(3):
            part = rest.astype(BF16)
            found += jnp.dot(selectors[1], part, preferred_element_type=F32)
            rest = rest - part.astype(F32)
        here = slot_scales.at[core, ring_x.pos]
        here[...] = found
        for peer in column_peers:
            slot_copies.append(wire.send(here, here, peer))
        return found

    small = [
        Trade(
            wire, first[q],
            lambda p, q=q: normed.at[q],
            lambda k, q=q: gathered.at[q, second[q].pos, first[q].pos],
        )
        for q in range(FLOWS)
    ]
    large = [
        Gather(
            wire, second[q], way_of(q, core), gathered.at[q, second[q].pos],
            lambda p, q=q: gathered.at[q, p],
        )
        for q in range(FLOWS)
    ]
    entry = [
        Gather(wire, ring_x, x_way[q], picked.at[q], lambda p, q=q: rows_in.at[q, core, p])
        for q in range(FLOWS)
    ]
    paired = [[] for _ in range(FLOWS)]
    logit_parts = []

    def share(q, by, src=None):
        block = rows_in.at[q, core, ring_x.index(by)]
        paired[q].append(wire.send(block if src is None else src, block, pair))


    def widen(q):
        small[q].finish()
        large[q].start()

    def enter(q):
        large[q].finish()
        rows = gathered[q].reshape(RING * RING * 16, width)
        mine = jnp.dot(selectors[q % 2], rows, preferred_element_type=F32).astype(BF16)
        picked[q] = mine
        entry[q].start()
        share(q, 0, picked.at[q])
        rows_in[q, core, ring_x.pos] = mine
        logit_parts.append(
            lax.dot_general(
                mine, router_ref[:, cols[q]], (((1,), (1,)), ((), ())), preferred_element_type=F32
            )
        )

    def pass_on(q):
        entry[q].middle()
        share(q, -x_way[q])

    def arrive(q):
        entry[q].finish()
        share(q, x_way[q])
        share(q, 2)

    def absorb(q):
        if q == 1:
            own_scale.append(scale_slots())
        for copy in paired[q]:
            copy.wait_recv()
        if q == 0:
            late[0].wait()
            late[1].wait()
        for c in range(2):
            block = rows_in[q, c].reshape(RING * picked.shape[1], width)
            part = jnp.dot(block, wgu[cols[q], :], preferred_element_type=F32)
            if q == 0:
                total[c] = part
            else:
                total[c] += part

    waves(
        FLOWS // 2,
        [
            begin, lambda q: outer[q].middle(), turn, close, widen,
            lambda q: large[q].middle(), enter, pass_on, arrive, absorb,
        ],
    )

    for copy in slot_copies:
        copy.wait_recv()
    for c in range(2):
        scale = slot_scales[c].reshape(RING * picked.shape[1], slot_scales.shape[3])
        scale = jnp.concatenate([scale] * (half // scale.shape[1]), axis=1)
        gate = total[c, :, pl.ds(0, half)] * scale
        up = total[c, :, pl.ds(half, half)] * scale
        hidden[c] = (gate / (1.0 + jnp.exp(-gate)) * up).astype(BF16)
    late[2].wait()

    along = [Scatter(wire, ring_x, x_way[q], px.at[q], (x0, x1, x2, x3), q) for q in range(FLOWS)]
    outer_back, inner_back = plane_scatter()
    crossing = {}
    share_of = []

    def cross(q):
        part = jnp.dot(hidden[1 - core], wd[:, cols[q]], preferred_element_type=F32)
        away[q] = part.astype(BF16)
        crossing[q] = wire.send(away.at[q], from_pair.at[q], pair)

    def begin_back(q):
        part = jnp.dot(hidden[core], wd[:, cols[q]], preferred_element_type=F32)
        crossing[q].wait_recv()
        part = part + from_pair[q].astype(F32)
        px[q] = part.astype(BF16).reshape(RING, picked.shape[1], width)
        along[q].start()
        if q == 1:
            logits = sum(logit_parts) * own_scale[0][:, : router_ref.shape[0]]
            affinity = 1.0 / (1.0 + jnp.exp(-logits))
            column = lax.broadcasted_iota(jnp.int32, affinity.shape, 1)
            mine = jnp.sum(jnp.where(column == me_f, affinity, 0.0), axis=1, keepdims=True)
            both = jnp.sum(affinity * named[0], axis=1, keepdims=True)
            share_of.append(2.5 * mine / jnp.where(both > 0.0, both, 1.0))

    def combine(q):
        outer[q].settle()
        inner[q].settle()
        rows = along[q].finish().astype(BF16).astype(F32)
        rows = (rows * share_of[0]).astype(BF16)
        back = lax.dot_general(
            selectors[1 - q % 2], rows, (((0,), (0,)), ((), ())), preferred_element_type=F32
        )
        p1[q] = back.astype(BF16).reshape(RING, 64, width)
        outer_back[q].start()

    def turn_back(q):
        p2[q] = outer_back[q].finish().astype(BF16).reshape(RING, 16, width)
        inner_back[q].start()

    def close_back(q):
        out_ref[:, :, cols[q]] = inner_sum(q, inner_back[q]).reshape(8, 2, width).astype(BF16)

    waves(
        FLOWS // 2,
        [
            cross, begin_back, lambda q: along[q].middle(), combine,
            lambda q: outer_back[q].middle(), turn_back, close_back,
        ],
    )
    wire.drain()


def vmem_specs(count):
    return [pl.BlockSpec(memory_space=pltpu.VMEM)] * count


def exchange_bufs(rows, width):
    return [pltpu.VMEM((FLOWS, rows, width), BF16)] * 4


PIECE = 16
VMEM_LIMIT = 66 * 1024 * 1000
SENDS = 4


def attend_kernel(
    len_ref, hand_ref, q_hbm, kt_hbm, fresh_ref, w_ref,
    v_ref,
    flag_ref, q, kt, sent, got, flags, values, passed, send_sem, recv_sem, load_sem,
):
    _, ring_y, ring_z, _, _ = rings()
    a, f = lax.axis_index("attn"), lax.axis_index("ffn")
    count = lax.axis_size("attn")
    onward = {"attn": lax.rem(a + 1, count)}
    behind = {"attn": lax.rem(a + count - 1, count)}
    requests, rows, rank = q.shape[0], q.shape[1], w_ref.shape[1]
    heads = rows // 2
    loads = []
    for r in range(requests):
        pair = (
            pltpu.make_async_copy(q_hbm.at[r], q.at[r], load_sem.at[2 * r]),
            pltpu.make_async_copy(kt_hbm.at[r], kt.at[r], load_sem.at[2 * r + 1]),
        )
        for load in pair:
            load.start()
        loads.append(pair)
    offsets = [(dy, dz) for dy in (2, 1, 3, 0) for dz in (2, 1, 3, 0) if (dy, dz) != (0, 0)]

    def peer(dy, dz):
        return ring_y.index(dy) * RING + ring_z.index(dz)

    token = lax.broadcasted_iota(jnp.int32, flag_ref.shape, 0) // 2
    flag = jnp.zeros(flag_ref.shape, F32)
    for r in range(requests):
        flag = jnp.where(token == r, hand_ref[0, r].astype(F32), flag)
    flag_ref[...] = flag.astype(BF16)
    flags[ring_y.pos, ring_z.pos] = flag.astype(BF16)
    meet([{"ffn": peer(dy, dz)} for dy, dz in offsets] + [onward, behind])
    wire = Wire(send_sem, recv_sem)
    flag_copies = {}
    for dy, dz in offsets:
        flag_copies[dy, dz] = wire.send(
            flag_ref, flags.at[ring_y.pos, ring_z.pos], {"ffn": peer(dy, dz)}
        )

    place = lax.broadcasted_iota(jnp.int32, (2 * rows, 2 * rows), 0)
    source = lax.broadcasted_iota(jnp.int32, (2 * rows, 2 * rows), 1)
    wanted = (
        (place % 16) // 8 * rows + (place % 8) // 4 * heads + place // 16 * 4 + place % 4
    )
    order = (source == wanted).astype(F32).astype(BF16)
    position = lax.broadcasted_iota(jnp.int32, (rows, kt.shape[2]), 1)
    step = lax.broadcasted_iota(jnp.int32, (rows, fresh_ref.shape[1]), 0) // heads
    column = lax.broadcasted_iota(jnp.int32, (rows, fresh_ref.shape[1]), 1)
    across = (((1,), (1,)), ((), ()))

    def attend(r):
        old = jnp.dot(q[r], kt[r], preferred_element_type=F32) * score_scale
        old = jnp.where(position < len_ref[r], old, -jnp.inf)
        new = lax.dot_general(q[r], fresh_ref[r], across, preferred_element_type=F32) * score_scale
        new = jnp.where(column <= step, new, -jnp.inf)
        peak = jnp.maximum(
            jnp.max(old, axis=1, keepdims=True), jnp.max(new, axis=1, keepdims=True)
        )
        old, new = jnp.exp(old - peak), jnp.exp(new - peak)
        below = jnp.sum(old, axis=1, keepdims=True) + jnp.sum(new, axis=1, keepdims=True)
        mixed = lax.dot_general(
            (old / below).astype(BF16), kt[r, pl.ds(0, rank), :], across, preferred_element_type=F32
        )
        mixed = mixed + jnp.dot(
            (new / below).astype(BF16), fresh_ref[r, :, pl.ds(0, rank)], preferred_element_type=F32
        )
        return mixed.astype(BF16)

    pairs = requests // 2
    per_send = pairs // SENDS
    copies = {}
    for p in range(pairs):
        for load in loads[2 * p] + loads[2 * p + 1]:
            load.wait()
        both = jnp.concatenate([attend(2 * p), attend(2 * p + 1)], axis=0)
        piece = jnp.dot(order, both, preferred_element_type=F32).astype(BF16)
        sent[:, p] = piece.reshape(RING * RING, PIECE, rank)
        if (p + 1) % per_send == 0:
            part = pl.ds(p + 1 - per_send, per_send)
            for dy, dz in offsets:
                to = peer(dy, dz)
                copies.setdefault(dy, []).append(
                    wire.send(sent.at[to, part], got.at[ring_y.pos, ring_z.pos, part], {"ffn": to})
                )
    got[ring_y.pos, ring_z.pos] = sent[f]

    block_rows = RING * pairs * PIECE
    tokens = block_rows // 4
    gather = (
        lax.broadcasted_iota(jnp.int32, (tokens, block_rows), 1) // 4
        == lax.broadcasted_iota(jnp.int32, (tokens, block_rows), 0)
    ).astype(F32).astype(BF16)
    head = lax.broadcasted_iota(jnp.int32, (block_rows, w_ref.shape[2]), 0) % 4
    shifts = {}
    turns = (0, 1, 3, 2)
    for dy in turns:
        for copy in copies[dy]:
            copy.wait_recv()
        block = ring_y.index(-dy)
        latents = got[block].reshape(block_rows, rank)
        mapped = [
            jnp.where(
                head == j, jnp.dot(latents, w_ref[j], preferred_element_type=F32), 0.0
            ).astype(BF16)
            for j in range(w_ref.shape[0])
        ]
        value = jnp.dot(gather, jnp.concatenate(mapped, axis=1), preferred_element_type=F32)
        values[block] = value.astype(BF16)
        shifts[dy] = wire.send(values.at[block], passed.at[block], onward)
    for dy, dz in offsets:
        flag_copies[dy, dz].wait_recv()
    for dy in turns:
        shifts[dy].wait_recv()
        block = ring_y.index(-dy)
        flag = flags[block].reshape(tokens, flag_ref.shape[1]).astype(F32)
        moved = jnp.concatenate([flag] * (values.shape[2] // flag.shape[1]), axis=1) > 0.5
        v_ref[block] = jnp.where(moved, passed[block].astype(F32), values[block].astype(F32)).astype(BF16)
    wire.drain()


def attend(queries, cache, fresh, lengths, handoff, value_up):
    requests, steps, heads, latent = queries.shape
    span = cache.shape[1]
    per_dev, rank, v_head = value_up.shape
    rows = steps * heads
    plane = RING * RING
    copies = (plane - 1) * (1 + SENDS) + RING
    tokens = RING * requests * steps
    return pl.pallas_call(
        attend_kernel,
        name="attend",
        out_shape=jax.ShapeDtypeStruct((RING, tokens, per_dev * v_head), BF16),
        in_specs=[pl.BlockSpec(memory_space=pltpu.SMEM)] * 2
        + [pl.BlockSpec(memory_space=pl.ANY)] * 2
        + vmem_specs(2),
        out_specs=vmem_specs(1)[0],
        scratch_shapes=[
            pltpu.VMEM((requests * steps, 128), BF16),
            pltpu.VMEM((requests, rows, latent), BF16),
            pltpu.VMEM((requests, latent, span), BF16),
            pltpu.VMEM((plane, requests // 2, PIECE, rank), BF16),
            pltpu.VMEM((RING, RING, requests // 2, PIECE, rank), BF16),
            pltpu.VMEM((RING, RING, requests * steps, 128), BF16),
            pltpu.VMEM((RING, tokens, per_dev * v_head), BF16),
            pltpu.VMEM((RING, tokens, per_dev * v_head), BF16),
            pltpu.SemaphoreType.DMA((copies,)),
            pltpu.SemaphoreType.DMA((copies,)),
            pltpu.SemaphoreType.DMA((2 * requests,)),
        ],
        compiler_params=pltpu.CompilerParams(collective_id=3, has_side_effects=True),
    )(
        lengths,
        handoff,
        queries.reshape(requests, rows, latent),
        jnp.swapaxes(cache, 1, 2),
        fresh,
        value_up,
    )


def layer(v, output_weight, gate, up, down, residual, norm_gain, router_t, ids):
    depth, model_width = output_weight.shape
    width = model_width // FLOWS
    half = down.shape[0]
    tokens, slots = v.shape[0], 8 * residual.shape[0]
    copies = (12 + 7 + 1 + 9) * FLOWS + 15 + 7
    return pl.pallas_call(
        layer_kernel,
        name="layer",
        out_shape=(
            jax.ShapeDtypeStruct(residual.shape, BF16),
            jax.ShapeDtypeStruct(residual.shape, BF16),
        ),
        in_specs=vmem_specs(1) + [pl.BlockSpec(memory_space=pl.ANY)] * 4 + vmem_specs(4),
        out_specs=tuple(vmem_specs(2)),
        scratch_shapes=[
            pltpu.VMEM((tokens, depth), BF16),
            pltpu.VMEM((depth, model_width), BF16),
            pltpu.VMEM((model_width, 2 * half), BF16),
            pltpu.VMEM((half, model_width), BF16),
            pltpu.VMEM((FLOWS, 16, width), BF16),
            pltpu.VMEM((RING, RING, 16, 128), F32),
            pltpu.VMEM((FLOWS, RING, RING, 16, width), BF16),
            pltpu.VMEM((FLOWS, slots, width), BF16),
            pltpu.VMEM((2, slots, tokens), BF16),
            pltpu.VMEM((2, RING, slots, 128), F32),
            pltpu.VMEM((FLOWS, 2, RING, slots, width), BF16),
            pltpu.VMEM((2, RING * slots, 2 * half), F32),
            pltpu.VMEM((2, RING * slots, half), BF16),
            pltpu.VMEM((FLOWS, RING * slots, width), BF16),
            pltpu.VMEM((FLOWS, RING * slots, width), BF16),
            pltpu.VMEM((FLOWS, RING, slots, width), BF16),
            pltpu.VMEM((FLOWS, RING, 64, width), BF16),
            pltpu.VMEM((FLOWS, RING, 16, width), BF16),
            *exchange_bufs(slots, width),
            *exchange_bufs(64, width),
            *exchange_bufs(16, width)[1:],
            pltpu.SemaphoreType.DMA((copies,)),
            pltpu.SemaphoreType.DMA((copies,)),
            pltpu.SemaphoreType.DMA((FLOWS + 3,)),
        ],
        compiler_params=pltpu.CompilerParams(
            collective_id=1, has_side_effects=True, vmem_limit_bytes=VMEM_LIMIT
        ),
    )(v, output_weight, gate, up, down, residual, norm_gain, router_t, ids)


def local(
    queries,
    latent_cache,
    fresh_latent,
    lengths,
    handoff,
    residual,
    value_up_matrix,
    output_weight,
    norm_gain,
    router,
    expert_ids,
    gate_weight,
    up_weight,
    down_weight,
):
    heads_local, _, v_head = value_up_matrix.shape
    req_dev, steps_here, model_width = residual.shape
    row_tokens = expert_ids.shape[0] * steps_here
    value_rows = attend(queries, latent_cache, fresh_latent, lengths, handoff, value_up_matrix)
    attended, summed = layer(
        value_rows.reshape(row_tokens, heads_local * v_head),
        output_weight,
        gate_weight[0],
        up_weight[0],
        down_weight[0],
        residual,
        norm_gain.reshape(1, model_width),
        router.T,
        jnp.transpose(expert_ids, (1, 2, 0)).reshape(-1, expert_ids.shape[0]),
    )
    return (attended, summed)


def solution(mesh):
    return jax.shard_map(
        local,
        mesh=mesh,
        in_specs=(
            P(("attn", "ffn"), None, None, None),
            P(("attn", "ffn"), None, None),
            P(("attn", "ffn"), None, None),
            P(("attn", "ffn")),
            P("ffn", None),
            P(("attn", "ffn"), None, None),
            P("ffn", None, None),
            P("ffn", None),
            P(),
            P(),
            P("attn", None, None),
            P("ffn", None, "attn"),
            P("ffn", None, "attn"),
            P("ffn", "attn", None),
        ),
        out_specs=(P(("attn", "ffn"), None, None), P(("attn", "ffn"), None, None)),
        check_vma=False,
    )
```
